32 devices in a mesh: expert: 4 (over y, x), dp: 8 (over z, core).
Axes of the slice: x: 2, y: 2, z: 4, core: 2. Of those that a mesh axis runs over, the one named last changes fastest.
Arguments:
- tokens: bfloat16 [1024, 5120], P('dp', 'expert'), may hold values from -6 to 6
- routes: int32 [1024, 2], P('dp'), may hold values from 0 to 7, all different within a row; in each aligned block of 128 rows (0 to 127, 128 to 255, ...) at most 48 rows name the same one
- combine: bfloat16 [1024, 2], P('dp'), may hold values from 0.099609375 to 1
- cotangent: bfloat16 [1024, 5120], P('dp', 'expert'), may hold values from -1.5 to 1.5
- w_gate: bfloat16 [8, 5120, 768], P('dp', 'expert'), may hold values from -0.078125 to 0.078125
- w_up: bfloat16 [8, 5120, 768], P('dp', 'expert'), may hold values from -0.078125 to 0.078125
- w_down: bfloat16 [8, 768, 5120], P('dp', None, 'expert'), may hold values from -0.21875 to 0.21875
Outputs:
- token_grad: bfloat16 [1024, 5120], P('dp', 'expert')
- combine_grad: float32 [1024, 2], P('dp')
- grad_gate: bfloat16 [8, 5120, 768], P('dp', 'expert')
- grad_up: bfloat16 [8, 5120, 768], P('dp', 'expert')
- grad_down: bfloat16 [8, 768, 5120], P('dp', None, 'expert')
The draws below stay inside these ranges and needn't reach their ends.
Inputs may be any that keep to these rules, and one draw needn't show every extreme that they name: `routes`: each token names 2 different experts. The tokens of one group name any one expert at most 48 times, a bound that some block reaches.
All inputs are finite; a program needn't handle non-finite values.
Results may differ from the reference program's by a relative error of at most 0.018.
Values may be sent and summed in bfloat16 or wider, within the bound.
No kernel may reach another device: no remote copies, remote signals or barrier semaphores. Data moves between devices by JAX's collectives and lax.ppermute only.
A program may use at most 64 MiB of HBM per device.

```python
import math
import jax
import jax.numpy as jnp
import numpy as np
from jax import lax

D = 5120
H = 768
TOPK = 2
TOK_DEV = 128
EXPERTS = 8
CAP = 48
TOKENS = 1024
N_EXPERT = 4
N_DP = 8


def block_scale(key, extent, pieces, smallest, high):
    level, own = 1.0, jax.random.fold_in(key, 6)
    for dim, shards_of in pieces:
        steps = jnp.exp(jax.random.uniform(jax.random.fold_in(own, dim), (shards_of,), jnp.float32, smallest / len(pieces), high / len(pieces)))
        level = level * jnp.repeat(steps, extent[dim] // shards_of).reshape([-1 if axis == dim else 1 for axis in range(len(extent))])
    return level


def assign_block(stream_key, own, number, rows, count, top, bound, skew):
    order = jax.random.permutation(stream_key, count)
    heavy_load, common = portions_of(count, rows * top, bound, skew, True), portions_of(count, rows * top, bound, skew, False)
    places = jnp.arange(count)

    def named(sizes, offset_by):
        used = int((sizes > 0).sum())
        fixed = max(1, used // 4)
        shifted = fixed + (places - fixed + offset_by * (used - fixed)) % max(1, count - fixed)
        return jnp.zeros((count,), jnp.int32).at[order[jnp.where(places < fixed, places, shifted)]].set(jnp.asarray(sizes, jnp.int32))

    sizes = jnp.where(number % 4 == 0, named(heavy_load, number // 4), named(common, number - number // 4 - 1))
    mixed = jax.random.permutation(jax.random.fold_in(own, 3), count)
    donor, sink = mixed[0:count // 2 * 2:2], mixed[1:count // 2 * 2:2]
    slack = jnp.minimum(sizes[donor] - 1, bound - sizes[sink]) // 2
    slack = jnp.where((donor == order[0]) | (sink == order[0]) | (sizes[sink] == 0), 0, jnp.maximum(slack, 0))
    shifted = jax.random.randint(jax.random.fold_in(own, 4), (count // 2,), 0, 1 << 20) % (slack + 1)
    sizes = sizes.at[donor].add(-shifted).at[sink].add(shifted)
    items = jnp.searchsorted(jnp.cumsum(sizes), jnp.arange(rows * top), side="right").astype(jnp.int32)
    table = items.reshape(top, rows).T
    table = table[jax.random.permutation(jax.random.fold_in(own, 1), rows)]
    offset_by = jax.random.randint(jax.random.fold_in(own, 2), (rows, 1), 0, top)
    return jnp.take_along_axis(table, (jnp.arange(top)[None, :] + offset_by) % top, axis=1)


def portions_of(count, total, limit, skew, full):
    weights = [(1 << 20) // math.isqrt(standing ** skew) + 1 for standing in range(1, count + 1)]
    largest = limit if full else min(limit, max(-(-total // count), total * weights[0] // sum(weights)))
    least = 1 if total - largest >= count - 1 else 0
    given, surplus = [largest] + [least] * (count - 1), total - largest - least * (count - 1)
    while surplus > 0:
        movable = [i for i in range(1, count) if given[i] < largest] or [i for i in range(1, count) if given[i] < limit]
        mass, budget = sum([weights[i] for i in movable]), surplus
        for i in movable:
            more = min(limit - given[i], max(1, budget * weights[i] // mass), surplus)
            given[i] = given[i] + more
            surplus = surplus - more
    return np.array(given)


def noise(key, extent, scale, bound, split=(), kind=jnp.bfloat16):
    loudness = block_scale(key, extent, split, -0.22, 0.18) if split else 1.0
    array = jax.random.normal(key, extent, jnp.float32) * scale * loudness
    return jnp.minimum(jnp.maximum(array, -bound), bound).astype(kind)


def setup_inputs(seed: int = 0) -> dict:
    splits = jax.random.split(jax.random.key(seed), 8)
    tokens = noise(splits[0], (TOKENS, D), 1.0, 6.0, ((0, 8), (1, 4)))
    routes_keys = jax.random.split(jax.random.fold_in(splits[1], 1), TOKENS // TOK_DEV)
    routes_turns = jax.random.permutation(jax.random.fold_in(splits[1], 3), TOKENS // TOK_DEV)
    routes = jax.vmap(lambda own, number: assign_block(jax.random.fold_in(splits[1], 2), own, number, TOK_DEV, EXPERTS, TOPK, CAP, 2))(routes_keys, routes_turns).reshape((TOKENS, TOPK))
    combine = jnp.clip(0.099609375 + 0.9003906 * jax.random.uniform(splits[2], (TOKENS, TOPK), jnp.float32) ** block_scale(splits[2], (TOKENS, TOPK), ((0, 8),), -0.2, 0.2), 0.099609375, 1.0).astype(jnp.bfloat16)
    cotangent = noise(splits[3], (TOKENS, D), 0.25, 1.5, ((0, 8), (1, 4)))
    w_gate = noise(splits[4], (EXPERTS, D, H), D ** -0.5, 0.078125, ((0, 8), (1, 4)))
    w_up = noise(splits[5], (EXPERTS, D, H), D ** -0.5, 0.078125, ((0, 8), (1, 4)))
    w_down = noise(splits[6], (EXPERTS, H, D), H ** -0.5, 0.21875, ((0, 8), (2, 4)))
    return dict(tokens=tokens, routes=routes, combine=combine, cotangent=cotangent, w_gate=w_gate, w_up=w_up, w_down=w_down)


def contract_last(matrix_a, matrix_b):
    return lax.dot_general(matrix_a, matrix_b, (((1,), (1,)), ((), ())), preferred_element_type=jnp.float32)


def contract_first(matrix_a, matrix_b):
    return lax.dot_general(matrix_a, matrix_b, (((0,), (0,)), ((), ())), preferred_element_type=jnp.float32)


def swiglu_grads(pre_gate, pre_up, back_hidden, weights):
    sigmas = jax.nn.sigmoid(pre_gate)
    active = pre_gate * sigmas
    hidden = (active * pre_up).astype(jnp.bfloat16)
    scaled = weights[:, None] * back_hidden
    grad_gate_pre = (scaled * pre_up * sigmas * (1.0 + pre_gate * (1.0 - sigmas))).astype(jnp.bfloat16)
    grad_up_pre = (scaled * active).astype(jnp.bfloat16)
    return hidden, grad_gate_pre, grad_up_pre


def summed_rounded(partials):
    rounded = lax.optimization_barrier(partials.astype(jnp.bfloat16))
    return jnp.sum(rounded.astype(jnp.float32), axis=0)


def reference(tokens, routes, combine, cotangent, w_gate, w_up, w_down):
    per_block = TOK_DEV * TOPK
    block_routes = routes.reshape(N_DP, per_block)
    onehot = (block_routes[:, :, None] == jnp.arange(EXPERTS, dtype=jnp.int32)[None, None, :]).astype(jnp.int32)
    slot_rank = jnp.sum((jnp.cumsum(onehot, axis=1) - onehot) * onehot, axis=2).astype(jnp.int32)
    block_index = jnp.broadcast_to(jnp.arange(N_DP, dtype=jnp.int32)[:, None], (N_DP, per_block))
    route_ids = jnp.arange(TOKENS * TOPK, dtype=jnp.int32).reshape(N_DP, per_block)
    owner = jnp.full((EXPERTS, N_DP, CAP), TOKENS * TOPK, jnp.int32)
    owner = owner.at[block_routes, block_index, slot_rank].set(route_ids)
    owner = owner.reshape(EXPERTS, N_DP * CAP)
    padded_tok = jnp.concatenate([tokens, jnp.zeros((1, D), jnp.bfloat16)], axis=0)
    padded_cot = jnp.concatenate([cotangent, jnp.zeros((1, D), jnp.bfloat16)], axis=0)
    padded_comb = jnp.concatenate([combine.reshape(TOKENS * TOPK), jnp.zeros((1,), jnp.bfloat16)], axis=0)
    part_width = D // N_EXPERT

    def per_expert(carry, inputs):
        dx_total, comb_total = carry
        route_of_slot, gate_mat, up_mat, down_mat = inputs
        token_of_slot = route_of_slot // TOPK
        token_slots = padded_tok[token_of_slot]
        cot_slots = padded_cot[token_of_slot]
        comb_slots = padded_comb[route_of_slot].astype(jnp.float32)
        slot_total = token_slots.shape[0]
        pieces_x = token_slots.astype(jnp.float32).reshape(slot_total, N_EXPERT, part_width)
        pieces_dy = cot_slots.astype(jnp.float32).reshape(slot_total, N_EXPERT, part_width)
        gate_blocks = gate_mat.astype(jnp.float32).reshape(N_EXPERT, part_width, H)
        up_blocks = up_mat.astype(jnp.float32).reshape(N_EXPERT, part_width, H)
        down_blocks = down_mat.astype(jnp.float32).reshape(H, N_EXPERT, part_width)
        pre_gate = summed_rounded(jnp.einsum("mjd,jdh->jmh", pieces_x, gate_blocks))
        pre_up = summed_rounded(jnp.einsum("mjd,jdh->jmh", pieces_x, up_blocks))
        back_hidden = summed_rounded(jnp.einsum("mjd,hjd->jmh", pieces_dy, down_blocks))
        hidden, grad_gate_pre, grad_up_pre = swiglu_grads(pre_gate, pre_up, back_hidden, comb_slots)
        slot_comb = jnp.sum(hidden.astype(jnp.float32) * back_hidden, axis=1)
        slot_dx = contract_last(grad_gate_pre, gate_mat) + contract_last(grad_up_pre, up_mat)
        scaled_dy = (comb_slots[:, None] * cot_slots.astype(jnp.float32)).astype(jnp.bfloat16)
        gate_grad = contract_first(token_slots, grad_gate_pre).astype(jnp.bfloat16)
        up_grad = contract_first(token_slots, grad_up_pre).astype(jnp.bfloat16)
        down_grad = contract_first(hidden, scaled_dy).astype(jnp.bfloat16)
        dx_total = dx_total.at[token_of_slot].add(slot_dx)
        comb_total = comb_total.at[route_of_slot].add(slot_comb)
        return (dx_total, comb_total), (gate_grad, up_grad, down_grad)

    start = (jnp.zeros((TOKENS + 1, D), jnp.float32), jnp.zeros((TOKENS * TOPK + 1,), jnp.float32))
    finals, grads = lax.scan(per_expert, start, (owner, w_gate, w_up, w_down))
    dx_total, comb_total = finals
    token_grad = dx_total[:TOKENS].astype(jnp.bfloat16)
    combine_grad = comb_total[:TOKENS * TOPK].reshape(TOKENS, TOPK)
    return token_grad, combine_grad, grads[0], grads[1], grads[2]
```

```python
import functools
import jax
import jax.numpy as jnp
from jax import lax
from jax.experimental import pallas as pl
from jax.experimental.pallas import tpu as pltpu
from jax.sharding import PartitionSpec as P

F32 = jnp.float32
BF16 = jnp.bfloat16
LANES = 128


def contract_last(matrix_a, matrix_b):
    return lax.dot_general(
        matrix_a, matrix_b, (((1,), (1,)), ((), ())), preferred_element_type=F32
    )


def contract_first(matrix_a, matrix_b):
    return lax.dot_general(
        matrix_a, matrix_b, (((0,), (0,)), ((), ())), preferred_element_type=F32
    )


def swiglu_grads(pre_gate, pre_up, back_hidden, weights):
    sigmas = jax.nn.sigmoid(pre_gate)
    active = pre_gate * sigmas
    hidden = (active * pre_up).astype(BF16)
    scaled = weights[:, None] * back_hidden
    grad_gate_pre = (scaled * pre_up * sigmas * (1.0 + pre_gate * (1.0 - sigmas))).astype(BF16)
    grad_up_pre = (scaled * active).astype(BF16)
    return (hidden, grad_gate_pre, grad_up_pre)


def slot_masks(routes_ref, experts, capacity):
    me = lax.axis_index("dp")
    tok_rows = routes_ref.shape[1]
    expert_of_row = jnp.bitwise_xor(me, lax.broadcasted_iota(jnp.int32, (experts, tok_rows), 0))
    first = routes_ref[0:1, :] == expert_of_row
    second = routes_ref[1:2, :] == expert_of_row
    named = jnp.where(first, 1.0, 0.0) + jnp.where(second, 1.0, 0.0)
    before = jnp.where(
        lax.broadcasted_iota(jnp.int32, (tok_rows, tok_rows), 0)
        < lax.broadcasted_iota(jnp.int32, (tok_rows, tok_rows), 1),
        1.0,
        0.0,
    ).astype(BF16)
    rank = jnp.dot(named.astype(BF16), before, preferred_element_type=F32).astype(jnp.int32)
    rank = jnp.where(named > 0.5, rank, -1)
    place = lax.broadcasted_iota(jnp.int32, (capacity, tok_rows), 0)
    hits = [place == rank[k : k + 1, :] for k in range(experts)]
    return first, second, hits


def send_kernel(experts, capacity, routes_ref, combine_ref, tokens_ref, cot_ref, *out_refs):
    first, second, hits = slot_masks(routes_ref, experts, capacity)
    comb = combine_ref[...].astype(F32)
    scale = jnp.where(first, comb[0:1, :], 0.0) + jnp.where(second, comb[1:2, :], 0.0)
    tokens = tokens_ref[...]
    cot = cot_ref[...]
    for k in range(experts):
        pick = jnp.where(hits[k], 1.0, 0.0).astype(BF16)
        weigh = jnp.where(hits[k], scale[k : k + 1, :], 0.0).astype(BF16)
        out_refs[k][0:capacity, :] = jnp.dot(pick, tokens, preferred_element_type=F32).astype(BF16)
        out_refs[k][capacity:, :] = jnp.dot(weigh, cot, preferred_element_type=F32).astype(BF16)


def forward_kernel(blocks, capacity, *refs):
    block_refs = refs[:blocks]
    gate_ref, up_ref, down_ref, left_ref, right_ref = refs[blocks:]
    tok = jnp.concatenate([ref[0:capacity, :] for ref in block_refs], axis=0)
    cot = jnp.concatenate([ref[capacity:, :] for ref in block_refs], axis=0)
    half = blocks // 2 * capacity
    parts = (
        jnp.dot(tok, gate_ref[0], preferred_element_type=F32),
        jnp.dot(tok, up_ref[0], preferred_element_type=F32),
        contract_last(cot, down_ref[0]),
    )
    for i, part in enumerate(parts):
        rounded = part.astype(BF16)
        left_ref[i] = rounded[:half]
        right_ref[i] = rounded[half:]


def backward_kernel(blocks, capacity, u_ref, ur_ref, v_ref, vr_ref, gate_ref, up_ref, *refs):
    hid_ref, gg_ref, gu_ref = refs[:3]
    back_refs = refs[3 : 3 + blocks]
    step = pl.program_id(0)
    columns = gate_ref.shape[1]
    width = pl.num_programs(0) * columns
    half = blocks // 2 * capacity

    @pl.when(step == 0)
    def _():
        eye = lax.broadcasted_iota(jnp.int32, (capacity, LANES), 0) == lax.broadcasted_iota(
            jnp.int32, (capacity, LANES), 1
        )
        for side, (own_ref, got_ref) in enumerate(((u_ref, ur_ref), (v_ref, vr_ref))):
            for b in range(blocks // 2):
                lo, hi = b * capacity, (b + 1) * capacity
                pre_gate, pre_up, back_hidden = (
                    own_ref[i, lo:hi, :].astype(F32) + got_ref[i, lo:hi, :].astype(F32)
                    for i in range(3)
                )
                sigmas = jax.nn.sigmoid(pre_gate)
                active = pre_gate * sigmas
                hidden = (active * pre_up).astype(BF16)
                gg = back_hidden * pre_up * sigmas * (1.0 + pre_gate * (1.0 - sigmas))
                rows = slice(side * half + lo, side * half + hi)
                hid_ref[rows, :] = hidden
                gg_ref[rows, :] = gg.astype(BF16)
                gu_ref[rows, :] = (back_hidden * active).astype(BF16)
                comb = jnp.sum(hidden.astype(F32) * back_hidden, axis=1, keepdims=True)
                row = jnp.sum(jnp.where(eye, comb, 0.0), axis=0, keepdims=True)
                high = row.astype(BF16)
                low = (row - high.astype(F32)).astype(BF16)
                tail = jnp.concatenate(
                    [high.astype(F32), low.astype(F32), jnp.zeros((14, LANES), F32)], axis=0
                )
                k = side * (blocks // 2) + b
                base = width // LANES * capacity
                back_refs[k][base : base + 16, :] = tail.astype(BF16)

    dx = contract_last(gg_ref[...], gate_ref[0]) + contract_last(gu_ref[...], up_ref[0])
    dx = dx.astype(BF16)
    per = columns // LANES
    for k in range(blocks):
        part = dx[k * capacity : (k + 1) * capacity, :]
        stacked = jnp.concatenate(
            [part[:, c * LANES : (c + 1) * LANES] for c in range(per)], axis=0
        )
        start = pl.multiple_of(step * (per * capacity), per * capacity)
        back_refs[k][pl.ds(start, per * capacity), :] = stacked


def weight_kernel(blocks, capacity, chunks, *refs):
    block_refs = refs[:blocks]
    hid_refs = refs[blocks : blocks + chunks]
    gg_refs = refs[blocks + chunks : blocks + 2 * chunks]
    gu_refs = refs[blocks + 2 * chunks : blocks + 3 * chunks]
    gate_ref, up_ref, down_ref = refs[blocks + 3 * chunks :]
    tok = jnp.concatenate([ref[0:capacity, :] for ref in block_refs], axis=0)
    cot = jnp.concatenate([ref[capacity:, :] for ref in block_refs], axis=0)
    join = lambda part: jnp.concatenate([ref[...] for ref in part], axis=0)
    gate_ref[0] = contract_first(tok, join(gg_refs)).astype(BF16)
    up_ref[0] = contract_first(tok, join(gu_refs)).astype(BF16)
    down_ref[0] = contract_first(join(hid_refs), cot).astype(BF16)


def merge_kernel(experts, capacity, routes_ref, combine_ref, *refs):
    back_refs = refs[:experts]
    grad_ref, comb_ref = refs[experts:]
    first, second, hits = slot_masks(routes_ref, experts, capacity)
    picks = [jnp.where(hit, 1.0, 0.0).astype(BF16) for hit in hits]
    pick = jnp.concatenate(picks, axis=0)
    groups = grad_ref.shape[1] // LANES
    for c in range(groups):
        piece = jnp.concatenate(
            [ref[c * capacity : (c + 1) * capacity, :] for ref in back_refs], axis=0
        )
        grad_ref[:, c * LANES : (c + 1) * LANES] = contract_first(pick, piece).astype(BF16)
    total0 = jnp.zeros(first[0:1].shape, F32)
    total1 = total0
    for k in range(experts):
        tail = back_refs[k][groups * capacity : groups * capacity + 16, :][:, :capacity]
        seen = jnp.dot(tail, picks[k], preferred_element_type=F32)
        value = seen[0:1, :] + seen[1:2, :]
        total0 = total0 + jnp.where(first[k : k + 1, :], value, 0.0)
        total1 = total1 + jnp.where(second[k : k + 1, :], value, 0.0)
    comb = combine_ref[...].astype(F32)
    comb_ref[0:1, :] = total0 / comb[0:1, :]
    comb_ref[1:2, :] = total1 / comb[1:2, :]


def permuted(value, axis, flip):
    size = lax.axis_size(axis)
    return lax.ppermute(value, axis, [(i, i ^ flip) for i in range(size)])


def vmem(mib):
    return pltpu.CompilerParams(vmem_limit_bytes=mib * 1024 * 1024)


def shape_of(*dims, dtype=BF16):
    return jax.ShapeDtypeStruct(dims, dtype)


def run_forward(blocks, capacity, w_gate, w_up, w_down):
    count = len(blocks)
    rows, width = blocks[0].shape
    hidden = w_gate.shape[2]
    tile = 256
    half = count // 2 * capacity
    whole = pl.BlockSpec((rows, width), lambda j: (0, 0))
    column = pl.BlockSpec((1, width, tile), lambda j: (0, 0, j))
    out = pl.BlockSpec((3, half, tile), lambda j: (0, 0, j))
    return pl.pallas_call(
        functools.partial(forward_kernel, count, capacity),
        grid=(hidden // tile,),
        in_specs=[whole] * count
        + [column, column, pl.BlockSpec((1, tile, width), lambda j: (0, j, 0))],
        out_specs=[out, out],
        out_shape=[shape_of(3, half, hidden)] * 2,
        compiler_params=vmem(40),
        cost_estimate=pl.CostEstimate(
            flops=6 * count * capacity * width * hidden,
            bytes_accessed=6 * width * hidden,
            transcendentals=0,
        ),
    )(*blocks, w_gate, w_up, w_down)


def run_backward(sums, count, capacity, w_gate, w_up):
    _, width, hidden = w_gate.shape
    tile = 256
    half = count // 2 * capacity
    rows = count * capacity
    part = pl.BlockSpec((3, half, hidden), lambda j: (0, 0, 0))
    row = pl.BlockSpec((1, tile, hidden), lambda j: (0, j, 0))
    kept = pl.BlockSpec((rows, hidden), lambda j: (0, 0))
    length = width // LANES * capacity + 16
    return pl.pallas_call(
        functools.partial(backward_kernel, count, capacity),
        grid=(width // tile,),
        in_specs=[part] * 4 + [row, row],
        out_specs=[kept] * 3 + [pl.BlockSpec((length, LANES), lambda j: (0, 0))] * count,
        out_shape=[shape_of(rows, hidden)] * 3 + [shape_of(length, LANES)] * count,
        compiler_params=vmem(40),
        cost_estimate=pl.CostEstimate(
            flops=4 * rows * width * hidden,
            bytes_accessed=4 * width * hidden,
            transcendentals=rows * hidden,
        ),
    )(*sums, w_gate, w_up)


def run_weights(blocks, capacity, kept, hidden):
    count, chunks = len(blocks), len(kept)
    rows, width = blocks[0].shape
    tile = 256
    column = pl.BlockSpec((rows, tile), lambda j: (0, j))
    flat = [kept[c][i] for i in range(3) for c in range(chunks)]
    held = [pl.BlockSpec(value.shape, lambda j: (0, 0)) for value in flat]
    row = pl.BlockSpec((1, tile, hidden), lambda j: (0, j, 0))
    return pl.pallas_call(
        functools.partial(weight_kernel, count, capacity, chunks),
        grid=(width // tile,),
        in_specs=[column] * count + held,
        out_specs=[row, row, pl.BlockSpec((1, hidden, tile), lambda j: (0, 0, j))],
        out_shape=[shape_of(1, width, hidden)] * 2 + [shape_of(1, hidden, width)],
        compiler_params=vmem(40),
        cost_estimate=pl.CostEstimate(
            flops=6 * count * capacity * width * hidden,
            bytes_accessed=6 * width * hidden,
            transcendentals=0,
        ),
    )(*blocks, *flat)


def expert_total(left, right):
    add = lambda a, b: (a.astype(F32) + b.astype(F32)).astype(BF16)
    left_got = permuted(left, "expert", 1)
    right_got = permuted(right, "expert", 2)
    left_pair = add(left, left_got)
    right_pair = add(right, right_got)
    left_rest = permuted(left_pair, "expert", 2)
    right_rest = permuted(right_pair, "expert", 1)
    return left_pair, left_rest, right_pair, right_rest


def exchange_body(tokens, routes, combine, cotangent, w_gate, w_up, w_down):
    tok_rows, width = tokens.shape
    top_routes = routes.shape[1]
    experts = lax.axis_size("dp")
    capacity = 3 * tok_rows * top_routes // (2 * experts)
    hidden = w_gate.shape[2]
    routes_t, combine_t = routes.T, combine.T
    sends = pl.pallas_call(
        functools.partial(send_kernel, experts, capacity),
        out_shape=[shape_of(2 * capacity, width)] * experts,
        compiler_params=vmem(40),
    )(routes_t, combine_t, tokens, cotangent)
    order = [4, 5, 6, 7, 2, 3, 1]
    blocks = {0: sends[0]}
    for k in order:
        blocks[k] = permuted(sends[k], "dp", k)
    kept, backs = [], {}
    for chunk in ((0, 1, 2, 3), (4, 5), (6, 7)):
        left, right = run_forward([blocks[k] for k in chunk], capacity, w_gate, w_up, w_down)
        sums = expert_total(left, right)
        out = run_backward(sums, len(chunk), capacity, w_gate, w_up)
        kept.append(out[:3])
        for k, value in zip(chunk, out[3:]):
            backs[k] = value if k == 0 else permuted(value, "dp", k)
    grad_gate, grad_up, grad_down = run_weights(
        [blocks[k] for k in range(experts)], capacity, kept, hidden
    )
    token_grad, comb_grad = pl.pallas_call(
        functools.partial(merge_kernel, experts, capacity),
        out_shape=[shape_of(tok_rows, width), shape_of(top_routes, tok_rows, dtype=F32)],
        compiler_params=vmem(40),
    )(routes_t, combine_t, *[backs[k] for k in range(experts)])
    return (token_grad, comb_grad.T, grad_gate, grad_up, grad_down)


def gather_body(tokens, routes, combine, cotangent, w_gate, w_up, w_down):
    tok_rows, slice_width = tokens.shape
    top_routes = routes.shape[1]
    experts = lax.axis_size("dp")
    capacity = 3 * tok_rows * top_routes // (2 * experts)
    route_count = tok_rows * top_routes
    slot_total = experts * capacity
    route_flat = routes.reshape(route_count)
    onehot = (route_flat[:, None] == jnp.arange(experts, dtype=jnp.int32)[None, :]).astype(
        jnp.int32
    )
    slot_rank = jnp.sum((jnp.cumsum(onehot, axis=0) - onehot) * onehot, axis=1)
    places = route_flat * capacity + slot_rank
    source = jnp.full((slot_total,), route_count, jnp.int32)
    source = source.at[places].set(jnp.arange(route_count, dtype=jnp.int32))
    blank_row = jnp.zeros((1, slice_width), BF16)
    token_send = jnp.concatenate([tokens, blank_row], axis=0)[source // top_routes]
    cot_send = jnp.concatenate([cotangent, blank_row], axis=0)[source // top_routes]
    comb_send = jnp.concatenate(
        [combine.reshape(route_count), jnp.zeros((1,), BF16)], axis=0
    )[source]
    spread = functools.partial(
        lax.all_to_all, axis_name="dp", split_axis=0, concat_axis=0, tiled=True
    )
    token_slots = spread(token_send.reshape(experts, capacity, slice_width)).reshape(
        slot_total, slice_width
    )
    cot_slots = spread(cot_send.reshape(experts, capacity, slice_width)).reshape(
        slot_total, slice_width
    )
    comb_slots = spread(comb_send.reshape(experts, capacity)).reshape(slot_total).astype(F32)
    gate_mat, up_mat, down_mat = w_gate[0], w_up[0], w_down[0]
    partials = jnp.stack(
        [
            jnp.dot(token_slots, gate_mat, preferred_element_type=F32),
            jnp.dot(token_slots, up_mat, preferred_element_type=F32),
            contract_last(cot_slots, down_mat),
        ],
        axis=1,
    )
    summed = lax.psum_scatter(
        partials.astype(BF16), "expert", scatter_dimension=2, tiled=True
    ).astype(F32)
    hidden_part, gate_part, up_part = swiglu_grads(
        summed[:, 0], summed[:, 1], summed[:, 2], comb_slots
    )
    slot_comb = jnp.sum(hidden_part.astype(F32) * summed[:, 2], axis=1)
    joined = lax.all_gather(
        jnp.stack([hidden_part, gate_part, up_part], axis=1), "expert", axis=2, tiled=True
    )
    hidden, grad_gate_pre, grad_up_pre = joined[:, 0], joined[:, 1], joined[:, 2]
    slot_dx = contract_last(grad_gate_pre, gate_mat) + contract_last(grad_up_pre, up_mat)
    scaled_dy = (comb_slots[:, None] * cot_slots.astype(F32)).astype(BF16)
    grad_gate = contract_first(token_slots, grad_gate_pre).astype(BF16)[None]
    grad_up = contract_first(token_slots, grad_up_pre).astype(BF16)[None]
    grad_down = contract_first(hidden, scaled_dy).astype(BF16)[None]
    back_dx = spread(slot_dx.reshape(experts, capacity, slice_width).astype(BF16)).astype(F32)
    back_comb = spread(slot_comb.reshape(experts, capacity).astype(BF16)).astype(F32)
    route_dx = back_dx.reshape(slot_total, slice_width)[places].reshape(
        tok_rows, top_routes, slice_width
    )
    token_grad = jnp.sum(route_dx, axis=1).astype(BF16)
    comb_part = back_comb.reshape(slot_total)[places].reshape(tok_rows, top_routes)
    combine_grad = lax.psum(comb_part, "expert")
    return (token_grad, combine_grad, grad_gate, grad_up, grad_down)


def body(tokens, routes, combine, cotangent, w_gate, w_up, w_down):
    tok_rows, width = tokens.shape
    experts = lax.axis_size("dp")
    capacity = 3 * tok_rows * routes.shape[1] // (2 * experts)
    fits = (
        experts == 8
        and lax.axis_size("expert") == 4
        and routes.shape[1] == 2
        and tok_rows == LANES
        and capacity % 16 == 0
        and width % 256 == 0
        and w_gate.shape[2] % 256 == 0
    )
    run = exchange_body if fits else gather_body
    return run(tokens, routes, combine, cotangent, w_gate, w_up, w_down)


def solution(mesh):
    in_specs = (
        P("dp", "expert"),
        P("dp", None),
        P("dp", None),
        P("dp", "expert"),
        P("dp", "expert", None),
        P("dp", "expert", None),
        P("dp", None, "expert"),
    )
    out_specs = (
        P("dp", "expert"),
        P("dp", None),
        P("dp", "expert", None),
        P("dp", "expert", None),
        P("dp", None, "expert"),
    )
    return jax.shard_map(body, mesh=mesh, in_specs=in_specs, out_specs=out_specs, check_vma=False)
```

```python
import functools
import jax
import jax.numpy as jnp
from jax import lax
from jax.experimental import pallas as pl
from jax.experimental.pallas import tpu as pltpu
from jax.sharding import PartitionSpec as P

F32 = jnp.float32
BF16 = jnp.bfloat16
LANES = 128
NO_COST = pl.CostEstimate(flops=1, bytes_accessed=1, transcendentals=0)


def contract_last(matrix_a, matrix_b):
    return lax.dot_general(
        matrix_a, matrix_b, (((1,), (1,)), ((), ())), preferred_element_type=F32
    )


def contract_first(matrix_a, matrix_b):
    return lax.dot_general(
        matrix_a, matrix_b, (((0,), (0,)), ((), ())), preferred_element_type=F32
    )


def swiglu_grads(pre_gate, pre_up, back_hidden, weights):
    sigmas = jax.nn.sigmoid(pre_gate)
    active = pre_gate * sigmas
    hidden = (active * pre_up).astype(BF16)
    scaled = weights[:, None] * back_hidden
    grad_gate_pre = (scaled * pre_up * sigmas * (1.0 + pre_gate * (1.0 - sigmas))).astype(BF16)
    grad_up_pre = (scaled * active).astype(BF16)
    return (hidden, grad_gate_pre, grad_up_pre)


HBM = pltpu.MemorySpace.HBM


def slot_masks(routes, messages, capacity, experts):
    me = lax.axis_index("dp")
    tok_rows = routes.shape[1]
    row = lax.broadcasted_iota(jnp.int32, (len(messages), tok_rows), 0)
    expert = jnp.zeros((len(messages), tok_rows), jnp.int32)
    for k, (shift, flip) in enumerate(messages):
        target = lax.rem((me // 2) + shift, experts // 2) * 2 + jnp.bitwise_xor(me % 2, flip)
        expert = jnp.where(row == k, target, expert)
    first = routes[0:1, :] == expert
    second = routes[1:2, :] == expert
    named = jnp.where(first, 1.0, 0.0) + jnp.where(second, 1.0, 0.0)
    before = jnp.where(
        lax.broadcasted_iota(jnp.int32, (tok_rows, tok_rows), 0)
        < lax.broadcasted_iota(jnp.int32, (tok_rows, tok_rows), 1),
        1.0,
        0.0,
    ).astype(BF16)
    rank = jnp.dot(named.astype(BF16), before, preferred_element_type=F32).astype(jnp.int32)
    rank = jnp.where(named > 0.5, rank, -1)
    place = lax.broadcasted_iota(jnp.int32, (capacity, tok_rows), 0)
    hits = [place == rank[k : k + 1, :] for k in range(len(messages))]
    return first, second, hits


def send_kernel(messages, capacity, experts, routes_hbm, combine_hbm, tokens_hbm, cot_hbm, *refs):
    out_refs = refs[:-5]
    routes_ref, combine_ref, tokens_ref, cot_ref, sems = refs[-5:]
    pairs = (
        (routes_hbm, routes_ref),
        (combine_hbm, combine_ref),
        (tokens_hbm, tokens_ref),
        (cot_hbm, cot_ref),
    )
    copies = [pltpu.make_async_copy(a, b, sems.at[i]) for i, (a, b) in enumerate(pairs)]
    for copy in copies:
        copy.start()
    copies[0].wait()
    copies[1].wait()
    first, second, hits = slot_masks(routes_ref[...], messages, capacity, experts)
    comb = combine_ref[...].astype(F32)
    scale = jnp.where(first, comb[0:1, :], 0.0) + jnp.where(second, comb[1:2, :], 0.0)
    copies[2].wait()
    copies[3].wait()
    tokens = tokens_ref[...]
    cot = cot_ref[...]
    places = [(out, at) for out in out_refs for at in range(0, out.shape[0], 2 * capacity)]
    for k, (out, at) in enumerate(places):
        pick = jnp.where(hits[k], 1.0, 0.0).astype(BF16)
        weigh = jnp.where(hits[k], scale[k : k + 1, :], 0.0).astype(BF16)
        mid, end = at + capacity, at + 2 * capacity
        out[at:mid, :] = jnp.dot(pick, tokens, preferred_element_type=F32).astype(BF16)
        out[mid:end, :] = jnp.dot(weigh, cot, preferred_element_type=F32).astype(BF16)


def hold_kernel(*refs):
    sems = refs[-1]
    count = len(refs) // 2
    copies = [
        pltpu.make_async_copy(refs[i], refs[count + i], sems.at[i]) for i in range(count)
    ]
    for copy in copies:
        copy.start()
    for copy in copies:
        copy.wait()


def forward_kernel(blocks, capacity, tile, *refs):
    block_refs = refs[:blocks]
    weights = refs[blocks : blocks + 3]
    out_ref = refs[-1]
    tok = jnp.concatenate([ref[0:capacity, :] for ref in block_refs], axis=0)
    cot = jnp.concatenate([ref[capacity : 2 * capacity, :] for ref in block_refs], axis=0)

    def step(j, _):
        at = pl.ds(pl.multiple_of(j * tile, tile), tile)
        for i in range(3):
            if i < 2:
                part = jnp.dot(tok, weights[i][0, :, at], preferred_element_type=F32)
            else:
                part = contract_last(cot, weights[i][0, at, :])
            out_ref[i, :, at] = part.astype(BF16)
        return 0

    lax.fori_loop(0, out_ref.shape[2] // tile, step, 0)


def backward_kernel(blocks, capacity, tile, own_ref, got_ref, gate_ref, up_ref, *refs):
    out_refs = refs[-3 - blocks :]
    hid_ref, gg_ref, gu_ref = out_refs[:3]
    back_refs = out_refs[3:]
    width = gate_ref.shape[1]
    eye = lax.broadcasted_iota(jnp.int32, (capacity, LANES), 0) == lax.broadcasted_iota(
        jnp.int32, (capacity, LANES), 1
    )
    base = width // LANES * capacity
    for k in range(blocks):
        rows = slice(k * capacity, (k + 1) * capacity)
        pre_gate, pre_up, back_hidden = (
            own_ref[i, rows, :].astype(F32) + got_ref[i, rows, :].astype(F32) for i in range(3)
        )
        sigmas = jax.nn.sigmoid(pre_gate)
        active = pre_gate * sigmas
        hidden = (active * pre_up).astype(BF16)
        gg = back_hidden * pre_up * sigmas * (1.0 + pre_gate * (1.0 - sigmas))
        hid_ref[rows, :] = hidden
        gg_ref[rows, :] = gg.astype(BF16)
        gu_ref[rows, :] = (back_hidden * active).astype(BF16)
        comb = jnp.sum(hidden.astype(F32) * back_hidden, axis=1, keepdims=True)
        row = jnp.sum(jnp.where(eye, comb, 0.0), axis=0, keepdims=True)
        high = row.astype(BF16)
        low = (row - high.astype(F32)).astype(BF16)
        tail = jnp.concatenate(
            [high.astype(F32), low.astype(F32), jnp.zeros((14, LANES), F32)], axis=0
        )
        back_refs[k][base : base + 16, :] = tail.astype(BF16)
    gg, gu = gg_ref[...], gu_ref[...]
    per = tile // LANES

    def step(j, _):
        at = pl.ds(pl.multiple_of(j * tile, tile), tile)
        dx = contract_last(gg, gate_ref[0, at, :]) + contract_last(gu, up_ref[0, at, :])
        dx = dx.astype(BF16)
        start = pl.multiple_of(j * (per * capacity), per * capacity)
        for k in range(blocks):
            part = dx[k * capacity : (k + 1) * capacity, :]
            stacked = jnp.concatenate(
                [part[:, c * LANES : (c + 1) * LANES] for c in range(per)], axis=0
            )
            back_refs[k][pl.ds(start, per * capacity), :] = stacked
        return 0

    lax.fori_loop(0, width // tile, step, 0)


def weight_kernel(blocks, capacity, chunks, *refs):
    block_refs = refs[:blocks]
    hid_refs = refs[blocks : blocks + chunks]
    gg_refs = refs[blocks + chunks : blocks + 2 * chunks]
    gu_refs = refs[blocks + 2 * chunks : blocks + 3 * chunks]
    gate_ref, up_ref, down_ref = refs[blocks + 3 * chunks :]
    tok = jnp.concatenate([ref[0:capacity, :] for ref in block_refs], axis=0)
    cot = jnp.concatenate([ref[capacity : 2 * capacity, :] for ref in block_refs], axis=0)
    join = lambda part: jnp.concatenate([ref[...] for ref in part], axis=0)
    gate_ref[0] = contract_first(tok, join(gg_refs)).astype(BF16)
    up_ref[0] = contract_first(tok, join(gu_refs)).astype(BF16)
    down_ref[0] = contract_first(join(hid_refs), cot).astype(BF16)


def merge_kernel(messages, capacity, experts, early, *refs):
    routes_ref, combine_ref = refs[early : early + 2]
    back_refs = refs[early + 2 : -2]
    grad_ref, comb_ref = refs[-2:]
    first, second, hits = slot_masks(routes_ref[...], messages, capacity, experts)
    picks = [jnp.where(hit, 1.0, 0.0).astype(BF16) for hit in hits]
    pick = jnp.concatenate(picks, axis=0)
    groups = grad_ref.shape[1] // LANES
    for c in range(groups):
        piece = jnp.concatenate(
            [ref[c * capacity : (c + 1) * capacity, :] for ref in back_refs], axis=0
        )
        grad_ref[:, c * LANES : (c + 1) * LANES] = contract_first(pick, piece).astype(BF16)
    total0 = jnp.zeros((1, LANES), F32)
    total1 = total0
    for k in range(len(messages)):
        tail = back_refs[k][groups * capacity : groups * capacity + 16, :][:, :capacity]
        seen = jnp.dot(tail, picks[k], preferred_element_type=F32)
        value = seen[0:1, :] + seen[1:2, :]
        total0 = total0 + jnp.where(first[k : k + 1, :], value, 0.0)
        total1 = total1 + jnp.where(second[k : k + 1, :], value, 0.0)
    comb = combine_ref[...].astype(F32)
    comb_ref[0:1, :] = total0 / comb[0:1, :]
    comb_ref[1:2, :] = total1 / comb[1:2, :]


def crossed(value, flips):
    experts, slots = lax.axis_size("expert"), lax.axis_size("dp")
    pairs = [
        (e * slots + d, (e ^ flips[d % 2]) * slots + d)
        for e in range(experts)
        for d in range(slots)
    ]
    return lax.ppermute(value, ("expert", "dp"), pairs)


def moved(value, message, back=False):
    shift, flip = message
    size = lax.axis_size("dp")
    chips = size // 2
    pairs = [(i, (i // 2 + shift) % chips * 2 + (i % 2 ^ flip)) for i in range(size)]
    if back:
        pairs = sorted((b, a) for a, b in pairs)
    return lax.ppermute(value, "dp", pairs)


def vmem(mib):
    return pltpu.CompilerParams(vmem_limit_bytes=mib * 1024 * 1024)


def shape_of(*dims, dtype=BF16):
    return jax.ShapeDtypeStruct(dims, dtype)


def in_hbm(count):
    return [pl.BlockSpec(memory_space=HBM)] * count


def in_vmem(count):
    return [pl.BlockSpec(memory_space=pltpu.MemorySpace.VMEM)] * count


def anywhere(count):
    return [pl.BlockSpec(memory_space=pl.ANY)] * count


def run_hold(*weights):
    return pl.pallas_call(
        hold_kernel,
        in_specs=in_hbm(len(weights)),
        out_specs=in_vmem(len(weights)),
        out_shape=[shape_of(*value.shape) for value in weights],
        scratch_shapes=[pltpu.SemaphoreType.DMA((len(weights),))],
        compiler_params=vmem(16),
        cost_estimate=NO_COST,
    )(*weights)


def run_forward(blocks, capacity, weights, *earlier):
    count = len(blocks)
    _, width, hidden = weights[0].shape
    return pl.pallas_call(
        functools.partial(forward_kernel, count, capacity, 256),
        in_specs=in_vmem(count + 3) + anywhere(len(earlier)),
        out_specs=in_vmem(1)[0],
        out_shape=shape_of(3, count * capacity, hidden),
        compiler_params=vmem(24),
        cost_estimate=NO_COST,
    )(*blocks, *weights, *earlier)


def run_backward(sums, count, capacity, w_gate, w_up, *earlier):
    _, width, hidden = w_gate.shape
    rows = count * capacity
    length = width // LANES * capacity + 16
    return pl.pallas_call(
        functools.partial(backward_kernel, count, capacity, 256),
        in_specs=in_vmem(4) + anywhere(len(earlier)),
        out_specs=in_vmem(3 + count),
        out_shape=[shape_of(rows, hidden)] * 3 + [shape_of(length, LANES)] * count,
        compiler_params=vmem(24),
        cost_estimate=NO_COST,
    )(*sums, w_gate, w_up, *earlier)


def run_weights(blocks, capacity, kept, hidden):
    count, chunks = len(blocks), len(kept)
    width = blocks[0].shape[1]
    tile = 256
    column = pl.BlockSpec((2 * capacity, tile), lambda j: (0, j))
    flat = [kept[c][i] for i in range(3) for c in range(chunks)]
    held = [pl.BlockSpec(value.shape, lambda j: (0, 0)) for value in flat]
    row = pl.BlockSpec((1, tile, hidden), lambda j: (0, j, 0))
    return pl.pallas_call(
        functools.partial(weight_kernel, count, capacity, chunks),
        grid=(width // tile,),
        in_specs=[column] * count + held,
        out_specs=[row, row, pl.BlockSpec((1, hidden, tile), lambda j: (0, 0, j))],
        out_shape=[shape_of(1, width, hidden)] * 2 + [shape_of(1, hidden, width)],
        compiler_params=vmem(40),
        cost_estimate=NO_COST,
    )(*blocks, *flat)


def expert_total(part):
    got = crossed(part, (1, 2))
    pair = (part.astype(F32) + got.astype(F32)).astype(BF16)
    return pair, crossed(pair, (2, 1))


SHIFTS = (0, 1, 3, 2)
MESSAGES = tuple((shift, flip) for shift in SHIFTS for flip in (0, 1))


def exchange_body(tokens, routes, combine, cotangent, w_gate, w_up, w_down):
    tok_rows, width = tokens.shape
    top_routes = routes.shape[1]
    experts = lax.axis_size("dp")
    capacity = 3 * tok_rows * top_routes // (2 * experts)
    hidden = w_gate.shape[2]
    routes_t, combine_t = routes.T, combine.T
    chunks = len(SHIFTS)
    sends = pl.pallas_call(
        functools.partial(send_kernel, MESSAGES, capacity, experts),
        in_specs=in_hbm(4),
        out_specs=in_vmem(chunks + 1),
        out_shape=[shape_of(2 * capacity, width)] * 2
        + [shape_of(4 * capacity, width)] * (chunks - 1),
        scratch_shapes=[
            pltpu.VMEM(routes_t.shape, jnp.int32),
            pltpu.VMEM(combine_t.shape, BF16),
            pltpu.VMEM(tokens.shape, BF16),
            pltpu.VMEM(tokens.shape, BF16),
            pltpu.SemaphoreType.DMA((4,)),
        ],
        compiler_params=vmem(32),
        cost_estimate=NO_COST,
    )(routes_t, combine_t, tokens, cotangent)
    blocks = [(sends[0], moved(sends[1], (0, 1)))]
    for shift, value in zip(SHIFTS[1:], sends[2:]):
        whole = moved(value, (shift, 0))
        blocks.append((whole, moved(whole[2 * capacity :], (0, 1))))
    weights = run_hold(w_gate, w_up, w_down)
    sums, kept, backs = [], [], []

    def backward(i, *earlier):
        out = run_backward(sums[i], 2, capacity, *weights[:2], *earlier)
        kept.append(out[:3])
        for message, value in zip(MESSAGES[2 * i : 2 * i + 2], out[3:]):
            backs.append(value if message == (0, 0) else moved(value, message, back=True))

    for i, pair in enumerate(blocks):
        earlier = [done[0] for done in sums[-1:]] + [done[0] for done in kept[-1:]]
        part = run_forward(pair, capacity, weights, *earlier)
        sums.append(expert_total(part))
        if i:
            backward(i - 1, part)
    backward(chunks - 1, kept[-1][0])
    flat = [block for pair in blocks for block in pair]
    grad_gate, grad_up, grad_down = run_weights(flat, capacity, kept, hidden)
    token_grad, comb_grad = pl.pallas_call(
        functools.partial(merge_kernel, MESSAGES, capacity, experts, 0),
        in_specs=in_vmem(2 + experts),
        out_specs=in_vmem(2),
        out_shape=[shape_of(tok_rows, width), shape_of(top_routes, tok_rows, dtype=F32)],
        compiler_params=vmem(32),
        cost_estimate=NO_COST,
    )(routes_t, combine_t, *backs)
    return (token_grad, comb_grad.T, grad_gate, grad_up, grad_down)


def gather_body(tokens, routes, combine, cotangent, w_gate, w_up, w_down):
    tok_rows, slice_width = tokens.shape
    top_routes = routes.shape[1]
    experts = lax.axis_size("dp")
    capacity = 3 * tok_rows * top_routes // (2 * experts)
    route_count = tok_rows * top_routes
    slot_total = experts * capacity
    route_flat = routes.reshape(route_count)
    onehot = (route_flat[:, None] == jnp.arange(experts, dtype=jnp.int32)[None, :]).astype(
        jnp.int32
    )
    slot_rank = jnp.sum((jnp.cumsum(onehot, axis=0) - onehot) * onehot, axis=1)
    places = route_flat * capacity + slot_rank
    source = jnp.full((slot_total,), route_count, jnp.int32)
    source = source.at[places].set(jnp.arange(route_count, dtype=jnp.int32))
    blank_row = jnp.zeros((1, slice_width), BF16)
    token_send = jnp.concatenate([tokens, blank_row], axis=0)[source // top_routes]
    cot_send = jnp.concatenate([cotangent, blank_row], axis=0)[source // top_routes]
    comb_send = jnp.concatenate(
        [combine.reshape(route_count), jnp.zeros((1,), BF16)], axis=0
    )[source]
    spread = functools.partial(
        lax.all_to_all, axis_name="dp", split_axis=0, concat_axis=0, tiled=True
    )
    token_slots = spread(token_send.reshape(experts, capacity, slice_width)).reshape(
        slot_total, slice_width
    )
    cot_slots = spread(cot_send.reshape(experts, capacity, slice_width)).reshape(
        slot_total, slice_width
    )
    comb_slots = spread(comb_send.reshape(experts, capacity)).reshape(slot_total).astype(F32)
    gate_mat, up_mat, down_mat = w_gate[0], w_up[0], w_down[0]
    partials = jnp.stack(
        [
            jnp.dot(token_slots, gate_mat, preferred_element_type=F32),
            jnp.dot(token_slots, up_mat, preferred_element_type=F32),
            contract_last(cot_slots, down_mat),
        ],
        axis=1,
    )
    summed = lax.psum_scatter(
        partials.astype(BF16), "expert", scatter_dimension=2, tiled=True
    ).astype(F32)
    hidden_part, gate_part, up_part = swiglu_grads(
        summed[:, 0], summed[:, 1], summed[:, 2], comb_slots
    )
    slot_comb = jnp.sum(hidden_part.astype(F32) * summed[:, 2], axis=1)
    joined = lax.all_gather(
        jnp.stack([hidden_part, gate_part, up_part], axis=1), "expert", axis=2, tiled=True
    )
    hidden, grad_gate_pre, grad_up_pre = joined[:, 0], joined[:, 1], joined[:, 2]
    slot_dx = contract_last(grad_gate_pre, gate_mat) + contract_last(grad_up_pre, up_mat)
    scaled_dy = (comb_slots[:, None] * cot_slots.astype(F32)).astype(BF16)
    grad_gate = contract_first(token_slots, grad_gate_pre).astype(BF16)[None]
    grad_up = contract_first(token_slots, grad_up_pre).astype(BF16)[None]
    grad_down = contract_first(hidden, scaled_dy).astype(BF16)[None]
    back_dx = spread(slot_dx.reshape(experts, capacity, slice_width).astype(BF16)).astype(F32)
    back_comb = spread(slot_comb.reshape(experts, capacity).astype(BF16)).astype(F32)
    route_dx = back_dx.reshape(slot_total, slice_width)[places].reshape(
        tok_rows, top_routes, slice_width
    )
    token_grad = jnp.sum(route_dx, axis=1).astype(BF16)
    comb_part = back_comb.reshape(slot_total)[places].reshape(tok_rows, top_routes)
    combine_grad = lax.psum(comb_part, "expert")
    return (token_grad, combine_grad, grad_gate, grad_up, grad_down)


def body(tokens, routes, combine, cotangent, w_gate, w_up, w_down):
    tok_rows, width = tokens.shape
    experts = lax.axis_size("dp")
    capacity = 3 * tok_rows * routes.shape[1] // (2 * experts)
    fits = (
        experts == 8
        and lax.axis_size("expert") == 4
        and routes.shape[1] == 2
        and tok_rows == LANES
        and capacity % 16 == 0
        and width % 256 == 0
        and w_gate.shape[2] % 256 == 0
    )
    run = exchange_body if fits else gather_body
    return run(tokens, routes, combine, cotangent, w_gate, w_up, w_down)


def solution(mesh):
    in_specs = (
        P("dp", "expert"),
        P("dp", None),
        P("dp", None),
        P("dp", "expert"),
        P("dp", "expert", None),
        P("dp", "expert", None),
        P("dp", None, "expert"),
    )
    out_specs = (
        P("dp", "expert"),
        P("dp", None),
        P("dp", "expert", None),
        P("dp", "expert", None),
        P("dp", None, "expert"),
    )
    return jax.shard_map(body, mesh=mesh, in_specs=in_specs, out_specs=out_specs, check_vma=False)
```

```python
import functools
import jax
import jax.numpy as jnp
from jax import lax
from jax.experimental import pallas as pl
from jax.experimental.pallas import tpu as pltpu
from jax.sharding import PartitionSpec as P

F32 = jnp.float32
BF16 = jnp.bfloat16
LANES = 128
NO_COST = pl.CostEstimate(flops=1, bytes_accessed=1, transcendentals=0)


def contract_last(matrix_a, matrix_b):
    return lax.dot_general(
        matrix_a, matrix_b, (((1,), (1,)), ((), ())), preferred_element_type=F32
    )


def contract_first(matrix_a, matrix_b):
    return lax.dot_general(
        matrix_a, matrix_b, (((0,), (0,)), ((), ())), preferred_element_type=F32
    )


def swiglu_grads(pre_gate, pre_up, back_hidden, weights):
    sigmas = jax.nn.sigmoid(pre_gate)
    active = pre_gate * sigmas
    hidden = (active * pre_up).astype(BF16)
    scaled = weights[:, None] * back_hidden
    grad_gate_pre = (scaled * pre_up * sigmas * (1.0 + pre_gate * (1.0 - sigmas))).astype(BF16)
    grad_up_pre = (scaled * active).astype(BF16)
    return (hidden, grad_gate_pre, grad_up_pre)


HBM = pltpu.MemorySpace.HBM


def chip_after(chip, shift, chips):
    place = (chip ^ (chip >> 1)) + shift & chips - 1
    return place ^ (place >> 1)


def slot_masks(routes, messages, capacity, experts):
    me = lax.axis_index("dp")
    tok_rows = routes.shape[1]
    row = lax.broadcasted_iota(jnp.int32, (len(messages), tok_rows), 0)
    expert = jnp.zeros((len(messages), tok_rows), jnp.int32)
    for k, (shift, flip) in enumerate(messages):
        target = chip_after(me // 2, shift, experts // 2) * 2 + jnp.bitwise_xor(me % 2, flip)
        expert = jnp.where(row == k, target, expert)
    first = routes[0:1, :] == expert
    second = routes[1:2, :] == expert
    named = jnp.where(first, 1.0, 0.0) + jnp.where(second, 1.0, 0.0)
    before = jnp.where(
        lax.broadcasted_iota(jnp.int32, (tok_rows, tok_rows), 0)
        < lax.broadcasted_iota(jnp.int32, (tok_rows, tok_rows), 1),
        1.0,
        0.0,
    ).astype(BF16)
    rank = jnp.dot(named.astype(BF16), before, preferred_element_type=F32).astype(jnp.int32)
    rank = jnp.where(named > 0.5, rank, -1)
    place = lax.broadcasted_iota(jnp.int32, (capacity, tok_rows), 0)
    hits = [place == rank[k : k + 1, :] for k in range(len(messages))]
    return first, second, hits


def send_kernel(messages, capacity, experts, routes_hbm, combine_hbm, tokens_hbm, cot_hbm, *refs):
    out_refs = refs[:-5]
    routes_ref, combine_ref, tokens_ref, cot_ref, sems = refs[-5:]
    pairs = (
        (routes_hbm, routes_ref),
        (combine_hbm, combine_ref),
        (tokens_hbm, tokens_ref),
        (cot_hbm, cot_ref),
    )
    copies = [pltpu.make_async_copy(a, b, sems.at[i]) for i, (a, b) in enumerate(pairs)]
    for copy in copies:
        copy.start()
    copies[0].wait()
    copies[1].wait()
    first, second, hits = slot_masks(routes_ref[...], messages, capacity, experts)
    comb = combine_ref[...].astype(F32)
    scale = jnp.where(first, comb[0:1, :], 0.0) + jnp.where(second, comb[1:2, :], 0.0)
    copies[2].wait()
    copies[3].wait()
    tokens = tokens_ref[...]
    cot = cot_ref[...]
    places = [(out, at) for out in out_refs for at in range(0, out.shape[0], 2 * capacity)]
    for k, (out, at) in enumerate(places):
        pick = jnp.where(hits[k], 1.0, 0.0).astype(BF16)
        weigh = jnp.where(hits[k], scale[k : k + 1, :], 0.0).astype(BF16)
        mid, end = at + capacity, at + 2 * capacity
        out[at:mid, :] = jnp.dot(pick, tokens, preferred_element_type=F32).astype(BF16)
        out[mid:end, :] = jnp.dot(weigh, cot, preferred_element_type=F32).astype(BF16)


def hold_kernel(*refs):
    sems = refs[-1]
    count = len(refs) // 2
    copies = [
        pltpu.make_async_copy(refs[i], refs[count + i], sems.at[i]) for i in range(count)
    ]
    for copy in copies:
        copy.start()
    for copy in copies:
        copy.wait()


def forward_kernel(blocks, capacity, tile, *refs):
    block_refs = refs[:blocks]
    weights = refs[blocks : blocks + 3]
    out_ref = refs[-1]
    tok = jnp.concatenate([ref[0:capacity, :] for ref in block_refs], axis=0)
    cot = jnp.concatenate([ref[capacity : 2 * capacity, :] for ref in block_refs], axis=0)

    def step(j, _):
        at = pl.ds(pl.multiple_of(j * tile, tile), tile)
        for i in range(3):
            if i < 2:
                part = jnp.dot(tok, weights[i][0, :, at], preferred_element_type=F32)
            else:
                part = contract_last(cot, weights[i][0, at, :])
            out_ref[i, :, at] = part.astype(BF16)
        return 0

    lax.fori_loop(0, out_ref.shape[2] // tile, step, 0)


def backward_kernel(blocks, capacity, tile, own_ref, got_ref, gate_ref, up_ref, *refs):
    out_refs = refs[-3 - blocks :]
    hid_ref, gg_ref, gu_ref = out_refs[:3]
    back_refs = out_refs[3:]
    width = gate_ref.shape[1]
    eye = lax.broadcasted_iota(jnp.int32, (capacity, LANES), 0) == lax.broadcasted_iota(
        jnp.int32, (capacity, LANES), 1
    )
    base = width // LANES * capacity
    for k in range(blocks):
        rows = slice(k * capacity, (k + 1) * capacity)
        pre_gate, pre_up, back_hidden = (
            own_ref[i, rows, :].astype(F32) + got_ref[i, rows, :].astype(F32) for i in range(3)
        )
        sigmas = jax.nn.sigmoid(pre_gate)
        active = pre_gate * sigmas
        hidden = (active * pre_up).astype(BF16)
        gg = back_hidden * pre_up * sigmas * (1.0 + pre_gate * (1.0 - sigmas))
        hid_ref[rows, :] = hidden
        gg_ref[rows, :] = gg.astype(BF16)
        gu_ref[rows, :] = (back_hidden * active).astype(BF16)
        comb = jnp.sum(hidden.astype(F32) * back_hidden, axis=1, keepdims=True)
        row = jnp.sum(jnp.where(eye, comb, 0.0), axis=0, keepdims=True)
        high = row.astype(BF16)
        low = (row - high.astype(F32)).astype(BF16)
        tail = jnp.concatenate(
            [high.astype(F32), low.astype(F32), jnp.zeros((14, LANES), F32)], axis=0
        )
        back_refs[k][base : base + 16, :] = tail.astype(BF16)
    gg, gu = gg_ref[...], gu_ref[...]
    per = tile // LANES

    def step(j, _):
        at = pl.ds(pl.multiple_of(j * tile, tile), tile)
        dx = contract_last(gg, gate_ref[0, at, :]) + contract_last(gu, up_ref[0, at, :])
        dx = dx.astype(BF16)
        start = pl.multiple_of(j * (per * capacity), per * capacity)
        for k in range(blocks):
            part = dx[k * capacity : (k + 1) * capacity, :]
            stacked = jnp.concatenate(
                [part[:, c * LANES : (c + 1) * LANES] for c in range(per)], axis=0
            )
            back_refs[k][pl.ds(start, per * capacity), :] = stacked
        return 0

    lax.fori_loop(0, width // tile, step, 0)


def weight_kernel(blocks, capacity, chunks, *refs):
    block_refs = refs[:blocks]
    hid_refs = refs[blocks : blocks + chunks]
    gg_refs = refs[blocks + chunks : blocks + 2 * chunks]
    gu_refs = refs[blocks + 2 * chunks : blocks + 3 * chunks]
    gate_ref, up_ref, down_ref = refs[blocks + 3 * chunks :]
    tok = jnp.concatenate([ref[0:capacity, :] for ref in block_refs], axis=0)
    cot = jnp.concatenate([ref[capacity : 2 * capacity, :] for ref in block_refs], axis=0)
    join = lambda part: jnp.concatenate([ref[...] for ref in part], axis=0)
    gate_ref[0] = contract_first(tok, join(gg_refs)).astype(BF16)
    up_ref[0] = contract_first(tok, join(gu_refs)).astype(BF16)
    down_ref[0] = contract_first(join(hid_refs), cot).astype(BF16)


def merge_kernel(messages, capacity, experts, early, *refs):
    routes_ref, combine_ref = refs[early : early + 2]
    back_refs = refs[early + 2 : -2]
    grad_ref, comb_ref = refs[-2:]
    first, second, hits = slot_masks(routes_ref[...], messages, capacity, experts)
    picks = [jnp.where(hit, 1.0, 0.0).astype(BF16) for hit in hits]
    pick = jnp.concatenate(picks, axis=0)
    groups = grad_ref.shape[1] // LANES
    for c in range(groups):
        piece = jnp.concatenate(
            [ref[c * capacity : (c + 1) * capacity, :] for ref in back_refs], axis=0
        )
        grad_ref[:, c * LANES : (c + 1) * LANES] = contract_first(pick, piece).astype(BF16)
    total0 = jnp.zeros((1, LANES), F32)
    total1 = total0
    for k in range(len(messages)):
        tail = back_refs[k][groups * capacity : groups * capacity + 16, :][:, :capacity]
        seen = jnp.dot(tail, picks[k], preferred_element_type=F32)
        value = seen[0:1, :] + seen[1:2, :]
        total0 = total0 + jnp.where(first[k : k + 1, :], value, 0.0)
        total1 = total1 + jnp.where(second[k : k + 1, :], value, 0.0)
    comb = combine_ref[...].astype(F32)
    comb_ref[0:1, :] = total0 / comb[0:1, :]
    comb_ref[1:2, :] = total1 / comb[1:2, :]


def crossed(value, flips):
    experts, slots = lax.axis_size("expert"), lax.axis_size("dp")
    pairs = [
        (e * slots + d, (e ^ flips[d % 2]) * slots + d)
        for e in range(experts)
        for d in range(slots)
    ]
    return lax.ppermute(value, ("expert", "dp"), pairs)


def moved(value, message, back=False):
    shift, flip = message
    size = lax.axis_size("dp")
    chips = size // 2
    pairs = [(i, chip_after(i // 2, shift, chips) * 2 + (i % 2 ^ flip)) for i in range(size)]
    if back:
        pairs = sorted((b, a) for a, b in pairs)
    return lax.ppermute(value, "dp", pairs)


def vmem(mib):
    return pltpu.CompilerParams(vmem_limit_bytes=mib * 1024 * 1024)


def shape_of(*dims, dtype=BF16):
    return jax.ShapeDtypeStruct(dims, dtype)


def in_hbm(count):
    return [pl.BlockSpec(memory_space=HBM)] * count


def in_vmem(count):
    return [pl.BlockSpec(memory_space=pltpu.MemorySpace.VMEM)] * count


def kept_in_hbm(value):
    return pltpu.with_memory_space_constraint(value, HBM)


def anywhere(count):
    return [pl.BlockSpec(memory_space=pl.ANY)] * count


def run_hold(*weights):
    return pl.pallas_call(
        hold_kernel,
        in_specs=in_hbm(len(weights)),
        out_specs=in_vmem(len(weights)),
        out_shape=[shape_of(*value.shape) for value in weights],
        scratch_shapes=[pltpu.SemaphoreType.DMA((len(weights),))],
        compiler_params=vmem(16),
        cost_estimate=NO_COST,
    )(*map(kept_in_hbm, weights))


def run_forward(blocks, capacity, weights, *earlier):
    count = len(blocks)
    _, width, hidden = weights[0].shape
    return pl.pallas_call(
        functools.partial(forward_kernel, count, capacity, 256),
        in_specs=in_vmem(count + 3) + anywhere(len(earlier)),
        out_specs=in_vmem(1)[0],
        out_shape=shape_of(3, count * capacity, hidden),
        compiler_params=vmem(24),
        cost_estimate=NO_COST,
    )(*blocks, *weights, *earlier)


def run_backward(sums, count, capacity, w_gate, w_up, *earlier):
    _, width, hidden = w_gate.shape
    rows = count * capacity
    length = width // LANES * capacity + 16
    return pl.pallas_call(
        functools.partial(backward_kernel, count, capacity, 256),
        in_specs=in_vmem(4) + anywhere(len(earlier)),
        out_specs=in_vmem(3 + count),
        out_shape=[shape_of(rows, hidden)] * 3 + [shape_of(length, LANES)] * count,
        compiler_params=vmem(24),
        cost_estimate=NO_COST,
    )(*sums, w_gate, w_up, *earlier)


def run_weights(blocks, capacity, kept, hidden):
    count, chunks = len(blocks), len(kept)
    width = blocks[0].shape[1]
    tile = 256
    column = pl.BlockSpec((2 * capacity, tile), lambda j: (0, j))
    flat = [kept[c][i] for i in range(3) for c in range(chunks)]
    held = [pl.BlockSpec(value.shape, lambda j: (0, 0)) for value in flat]
    row = pl.BlockSpec((1, tile, hidden), lambda j: (0, j, 0))
    return pl.pallas_call(
        functools.partial(weight_kernel, count, capacity, chunks),
        grid=(width // tile,),
        in_specs=[column] * count + held,
        out_specs=[row, row, pl.BlockSpec((1, hidden, tile), lambda j: (0, 0, j))],
        out_shape=[shape_of(1, width, hidden)] * 2 + [shape_of(1, hidden, width)],
        compiler_params=vmem(40),
        cost_estimate=NO_COST,
    )(*blocks, *flat)


def expert_total(part):
    got = crossed(part, (1, 2))
    pair = (part.astype(F32) + got.astype(F32)).astype(BF16)
    return pair, crossed(pair, (2, 1))


SHIFTS = (0, 1, 3, 2)
MESSAGES = tuple((shift, flip) for shift in SHIFTS for flip in (0, 1))


def exchange_body(tokens, routes, combine, cotangent, w_gate, w_up, w_down):
    tok_rows, width = tokens.shape
    top_routes = routes.shape[1]
    experts = lax.axis_size("dp")
    capacity = 3 * tok_rows * top_routes // (2 * experts)
    hidden = w_gate.shape[2]
    routes_t, combine_t = routes.T, combine.T
    chunks = len(SHIFTS)
    sends = pl.pallas_call(
        functools.partial(send_kernel, MESSAGES, capacity, experts),
        in_specs=in_hbm(4),
        out_specs=in_vmem(chunks + 1),
        out_shape=[shape_of(2 * capacity, width)] * 2
        + [shape_of(4 * capacity, width)] * (chunks - 1),
        scratch_shapes=[
            pltpu.VMEM(routes_t.shape, jnp.int32),
            pltpu.VMEM(combine_t.shape, BF16),
            pltpu.VMEM(tokens.shape, BF16),
            pltpu.VMEM(tokens.shape, BF16),
            pltpu.SemaphoreType.DMA((4,)),
        ],
        compiler_params=vmem(32),
        cost_estimate=NO_COST,
    )(*map(kept_in_hbm, (routes_t, combine_t, tokens, cotangent)))
    blocks = [(sends[0], moved(sends[1], (0, 1)))]
    for shift, value in zip(SHIFTS[1:], sends[2:]):
        whole = moved(value, (shift, 0))
        blocks.append((whole, moved(whole[2 * capacity :], (0, 1))))
    weights = run_hold(w_gate, w_up, w_down)
    sums, kept, backs = [], [], []

    def backward(i, *earlier):
        out = run_backward(sums[i], 2, capacity, *weights[:2], *earlier)
        kept.append(out[:3])
        for message, value in zip(MESSAGES[2 * i : 2 * i + 2], out[3:]):
            backs.append(value if message == (0, 0) else moved(value, message, back=True))

    for i, pair in enumerate(blocks):
        earlier = [done[0] for done in sums[-1:]] + [done[0] for done in kept[-1:]]
        part = run_forward(pair, capacity, weights, *earlier)
        sums.append(expert_total(part))
        if i:
            backward(i - 1, part)
    backward(chunks - 1, kept[-1][0])
    flat = [block for pair in blocks for block in pair]
    grad_gate, grad_up, grad_down = run_weights(flat, capacity, kept, hidden)
    token_grad, comb_grad = pl.pallas_call(
        functools.partial(merge_kernel, MESSAGES, capacity, experts, 0),
        in_specs=in_vmem(2 + experts),
        out_specs=in_vmem(2),
        out_shape=[shape_of(tok_rows, width), shape_of(top_routes, tok_rows, dtype=F32)],
        compiler_params=vmem(32),
        cost_estimate=NO_COST,
    )(routes_t, combine_t, *backs)
    return (token_grad, comb_grad.T, grad_gate, grad_up, grad_down)


def gather_body(tokens, routes, combine, cotangent, w_gate, w_up, w_down):
    tok_rows, slice_width = tokens.shape
    top_routes = routes.shape[1]
    experts = lax.axis_size("dp")
    capacity = 3 * tok_rows * top_routes // (2 * experts)
    route_count = tok_rows * top_routes
    slot_total = experts * capacity
    route_flat = routes.reshape(route_count)
    onehot = (route_flat[:, None] == jnp.arange(experts, dtype=jnp.int32)[None, :]).astype(
        jnp.int32
    )
    slot_rank = jnp.sum((jnp.cumsum(onehot, axis=0) - onehot) * onehot, axis=1)
    places = route_flat * capacity + slot_rank
    source = jnp.full((slot_total,), route_count, jnp.int32)
    source = source.at[places].set(jnp.arange(route_count, dtype=jnp.int32))
    blank_row = jnp.zeros((1, slice_width), BF16)
    token_send = jnp.concatenate([tokens, blank_row], axis=0)[source // top_routes]
    cot_send = jnp.concatenate([cotangent, blank_row], axis=0)[source // top_routes]
    comb_send = jnp.concatenate(
        [combine.reshape(route_count), jnp.zeros((1,), BF16)], axis=0
    )[source]
    spread = functools.partial(
        lax.all_to_all, axis_name="dp", split_axis=0, concat_axis=0, tiled=True
    )
    token_slots = spread(token_send.reshape(experts, capacity, slice_width)).reshape(
        slot_total, slice_width
    )
    cot_slots = spread(cot_send.reshape(experts, capacity, slice_width)).reshape(
        slot_total, slice_width
    )
    comb_slots = spread(comb_send.reshape(experts, capacity)).reshape(slot_total).astype(F32)
    gate_mat, up_mat, down_mat = w_gate[0], w_up[0], w_down[0]
    partials = jnp.stack(
        [
            jnp.dot(token_slots, gate_mat, preferred_element_type=F32),
            jnp.dot(token_slots, up_mat, preferred_element_type=F32),
            contract_last(cot_slots, down_mat),
        ],
        axis=1,
    )
    summed = lax.psum_scatter(
        partials.astype(BF16), "expert", scatter_dimension=2, tiled=True
    ).astype(F32)
    hidden_part, gate_part, up_part = swiglu_grads(
        summed[:, 0], summed[:, 1], summed[:, 2], comb_slots
    )
    slot_comb = jnp.sum(hidden_part.astype(F32) * summed[:, 2], axis=1)
    joined = lax.all_gather(
        jnp.stack([hidden_part, gate_part, up_part], axis=1), "expert", axis=2, tiled=True
    )
    hidden, grad_gate_pre, grad_up_pre = joined[:, 0], joined[:, 1], joined[:, 2]
    slot_dx = contract_last(grad_gate_pre, gate_mat) + contract_last(grad_up_pre, up_mat)
    scaled_dy = (comb_slots[:, None] * cot_slots.astype(F32)).astype(BF16)
    grad_gate = contract_first(token_slots, grad_gate_pre).astype(BF16)[None]
    grad_up = contract_first(token_slots, grad_up_pre).astype(BF16)[None]
    grad_down = contract_first(hidden, scaled_dy).astype(BF16)[None]
    back_dx = spread(slot_dx.reshape(experts, capacity, slice_width).astype(BF16)).astype(F32)
    back_comb = spread(slot_comb.reshape(experts, capacity).astype(BF16)).astype(F32)
    route_dx = back_dx.reshape(slot_total, slice_width)[places].reshape(
        tok_rows, top_routes, slice_width
    )
    token_grad = jnp.sum(route_dx, axis=1).astype(BF16)
    comb_part = back_comb.reshape(slot_total)[places].reshape(tok_rows, top_routes)
    combine_grad = lax.psum(comb_part, "expert")
    return (token_grad, combine_grad, grad_gate, grad_up, grad_down)


def body(tokens, routes, combine, cotangent, w_gate, w_up, w_down):
    tok_rows, width = tokens.shape
    experts = lax.axis_size("dp")
    capacity = 3 * tok_rows * routes.shape[1] // (2 * experts)
    fits = (
        experts == 8
        and lax.axis_size("expert") == 4
        and routes.shape[1] == 2
        and tok_rows == LANES
        and capacity % 16 == 0
        and width % 256 == 0
        and w_gate.shape[2] % 256 == 0
    )
    run = exchange_body if fits else gather_body
    return run(tokens, routes, combine, cotangent, w_gate, w_up, w_down)


def solution(mesh):
    in_specs = (
        P("dp", "expert"),
        P("dp", None),
        P("dp", None),
        P("dp", "expert"),
        P("dp", "expert", None),
        P("dp", "expert", None),
        P("dp", None, "expert"),
    )
    out_specs = (
        P("dp", "expert"),
        P("dp", None),
        P("dp", "expert", None),
        P("dp", "expert", None),
        P("dp", None, "expert"),
    )
    return jax.shard_map(body, mesh=mesh, in_specs=in_specs, out_specs=out_specs, check_vma=False)
```

```python
import functools
import jax
import jax.numpy as jnp
from jax import lax
from jax.experimental import pallas as pl
from jax.experimental.pallas import tpu as pltpu
from jax.sharding import PartitionSpec as P

F32 = jnp.float32
BF16 = jnp.bfloat16
LANES = 128
NO_COST = pl.CostEstimate(flops=1, bytes_accessed=1, transcendentals=0)


def contract_last(matrix_a, matrix_b):
    return lax.dot_general(
        matrix_a, matrix_b, (((1,), (1,)), ((), ())), preferred_element_type=F32
    )


def contract_first(matrix_a, matrix_b):
    return lax.dot_general(
        matrix_a, matrix_b, (((0,), (0,)), ((), ())), preferred_element_type=F32
    )


def swiglu_grads(pre_gate, pre_up, back_hidden, weights):
    sigmas = jax.nn.sigmoid(pre_gate)
    active = pre_gate * sigmas
    hidden = (active * pre_up).astype(BF16)
    scaled = weights[:, None] * back_hidden
    grad_gate_pre = (scaled * pre_up * sigmas * (1.0 + pre_gate * (1.0 - sigmas))).astype(BF16)
    grad_up_pre = (scaled * active).astype(BF16)
    return (hidden, grad_gate_pre, grad_up_pre)


HBM = pltpu.MemorySpace.HBM


def chip_after(chip, shift, chips):
    place = (chip ^ (chip >> 1)) + shift & chips - 1
    return place ^ (place >> 1)


def slot_masks(routes, messages, capacity, experts):
    me = lax.axis_index("dp")
    tok_rows = routes.shape[1]
    row = lax.broadcasted_iota(jnp.int32, (len(messages), tok_rows), 0)
    expert = jnp.zeros((len(messages), tok_rows), jnp.int32)
    for k, (shift, flip) in enumerate(messages):
        target = chip_after(me // 2, shift, experts // 2) * 2 + jnp.bitwise_xor(me % 2, flip)
        expert = jnp.where(row == k, target, expert)
    first = routes[0:1, :] == expert
    second = routes[1:2, :] == expert
    named = jnp.where(first, 1.0, 0.0) + jnp.where(second, 1.0, 0.0)
    before = jnp.where(
        lax.broadcasted_iota(jnp.int32, (tok_rows, tok_rows), 0)
        < lax.broadcasted_iota(jnp.int32, (tok_rows, tok_rows), 1),
        1.0,
        0.0,
    ).astype(BF16)
    rank = jnp.dot(named.astype(BF16), before, preferred_element_type=F32).astype(jnp.int32)
    rank = jnp.where(named > 0.5, rank, -1)
    place = lax.broadcasted_iota(jnp.int32, (capacity, tok_rows), 0)
    hits = [place == rank[k : k + 1, :] for k in range(len(messages))]
    return first, second, hits


def send_kernel(messages, capacity, experts, routes_hbm, combine_hbm, tokens_hbm, cot_hbm, *refs):
    out_refs = refs[:-5]
    routes_ref, combine_ref, tokens_ref, cot_ref, sems = refs[-5:]
    pairs = (
        (routes_hbm, routes_ref),
        (combine_hbm, combine_ref),
        (tokens_hbm, tokens_ref),
        (cot_hbm, cot_ref),
    )
    copies = [pltpu.make_async_copy(a, b, sems.at[i]) for i, (a, b) in enumerate(pairs)]
    for copy in copies:
        copy.start()
    copies[0].wait()
    copies[1].wait()
    first, second, hits = slot_masks(routes_ref[...], messages, capacity, experts)
    comb = combine_ref[...].astype(F32)
    scale = jnp.where(first, comb[0:1, :], 0.0) + jnp.where(second, comb[1:2, :], 0.0)
    copies[2].wait()
    copies[3].wait()
    tokens = tokens_ref[...]
    cot = cot_ref[...]
    places = [(out, at) for out in out_refs for at in range(0, out.shape[0], 2 * capacity)]
    for k, (out, at) in enumerate(places):
        pick = jnp.where(hits[k], 1.0, 0.0).astype(BF16)
        weigh = jnp.where(hits[k], scale[k : k + 1, :], 0.0).astype(BF16)
        mid, end = at + capacity, at + 2 * capacity
        out[at:mid, :] = jnp.dot(pick, tokens, preferred_element_type=F32).astype(BF16)
        out[mid:end, :] = jnp.dot(weigh, cot, preferred_element_type=F32).astype(BF16)


def hold_kernel(*refs):
    sems = refs[-1]
    count = len(refs) // 2
    copies = [
        pltpu.make_async_copy(refs[i], refs[count + i], sems.at[i]) for i in range(count)
    ]
    for copy in copies:
        copy.start()
    for copy in copies:
        copy.wait()


def relay_kernel(rows, whole_ref, *refs):
    refs[-1][...] = whole_ref[rows:, :]


def forward_kernel(blocks, capacity, tile, *refs):
    block_refs = refs[:blocks]
    weights = refs[blocks : blocks + 3]
    out_ref = refs[-1]
    tok = jnp.concatenate([ref[0:capacity, :] for ref in block_refs], axis=0)
    cot = jnp.concatenate([ref[capacity : 2 * capacity, :] for ref in block_refs], axis=0)

    def step(j, _):
        at = pl.ds(pl.multiple_of(j * tile, tile), tile)
        for i in range(3):
            if i < 2:
                part = jnp.dot(tok, weights[i][0, :, at], preferred_element_type=F32)
            else:
                part = contract_last(cot, weights[i][0, at, :])
            out_ref[i, :, at] = part.astype(BF16)
        return 0

    lax.fori_loop(0, out_ref.shape[2] // tile, step, 0)


def backward_kernel(blocks, capacity, tile, own_ref, got_ref, gate_ref, up_ref, *refs):
    out_refs = refs[-3 - blocks :]
    hid_ref, gg_ref, gu_ref = out_refs[:3]
    back_refs = out_refs[3:]
    width = gate_ref.shape[1]
    eye = lax.broadcasted_iota(jnp.int32, (capacity, LANES), 0) == lax.broadcasted_iota(
        jnp.int32, (capacity, LANES), 1
    )
    base = width // LANES * capacity
    for k in range(blocks):
        rows = slice(k * capacity, (k + 1) * capacity)
        pre_gate, pre_up, back_hidden = (
            own_ref[i, rows, :].astype(F32) + got_ref[i, rows, :].astype(F32) for i in range(3)
        )
        sigmas = jax.nn.sigmoid(pre_gate)
        active = pre_gate * sigmas
        hidden = (active * pre_up).astype(BF16)
        gg = back_hidden * pre_up * sigmas * (1.0 + pre_gate * (1.0 - sigmas))
        hid_ref[rows, :] = hidden
        gg_ref[rows, :] = gg.astype(BF16)
        gu_ref[rows, :] = (back_hidden * active).astype(BF16)
        comb = jnp.sum(hidden.astype(F32) * back_hidden, axis=1, keepdims=True)
        row = jnp.sum(jnp.where(eye, comb, 0.0), axis=0, keepdims=True)
        high = row.astype(BF16)
        low = (row - high.astype(F32)).astype(BF16)
        tail = jnp.concatenate(
            [high.astype(F32), low.astype(F32), jnp.zeros((14, LANES), F32)], axis=0
        )
        back_refs[k][base : base + 16, :] = tail.astype(BF16)
    gg, gu = gg_ref[...], gu_ref[...]
    per = tile // LANES

    def step(j, _):
        at = pl.ds(pl.multiple_of(j * tile, tile), tile)
        dx = contract_last(gg, gate_ref[0, at, :]) + contract_last(gu, up_ref[0, at, :])
        dx = dx.astype(BF16)
        start = pl.multiple_of(j * (per * capacity), per * capacity)
        for k in range(blocks):
            part = dx[k * capacity : (k + 1) * capacity, :]
            stacked = jnp.concatenate(
                [part[:, c * LANES : (c + 1) * LANES] for c in range(per)], axis=0
            )
            back_refs[k][pl.ds(start, per * capacity), :] = stacked
        return 0

    lax.fori_loop(0, width // tile, step, 0)


def weight_kernel(blocks, capacity, chunks, *refs):
    block_refs = refs[:blocks]
    hid_refs = refs[blocks : blocks + chunks]
    gg_refs = refs[blocks + chunks : blocks + 2 * chunks]
    gu_refs = refs[blocks + 2 * chunks : blocks + 3 * chunks]
    gate_ref, up_ref, down_ref = refs[-3:]
    tok = jnp.concatenate([ref[0:capacity, :] for ref in block_refs], axis=0)
    cot = jnp.concatenate([ref[capacity : 2 * capacity, :] for ref in block_refs], axis=0)
    join = lambda part: jnp.concatenate([ref[...] for ref in part], axis=0)
    gate_ref[0] = contract_first(tok, join(gg_refs)).astype(BF16)
    up_ref[0] = contract_first(tok, join(gu_refs)).astype(BF16)
    down_ref[0] = contract_first(join(hid_refs), cot).astype(BF16)


def merge_kernel(messages, capacity, experts, early, *refs):
    routes_ref, combine_ref = refs[early : early + 2]
    back_refs = refs[early + 2 : -2]
    grad_ref, comb_ref = refs[-2:]
    first, second, hits = slot_masks(routes_ref[...], messages, capacity, experts)
    picks = [jnp.where(hit, 1.0, 0.0).astype(BF16) for hit in hits]
    pick = jnp.concatenate(picks, axis=0)
    groups = grad_ref.shape[1] // LANES
    for c in range(groups):
        piece = jnp.concatenate(
            [ref[c * capacity : (c + 1) * capacity, :] for ref in back_refs], axis=0
        )
        grad_ref[:, c * LANES : (c + 1) * LANES] = contract_first(pick, piece).astype(BF16)
    total0 = jnp.zeros((1, LANES), F32)
    total1 = total0
    for k in range(len(messages)):
        tail = back_refs[k][groups * capacity : groups * capacity + 16, :][:, :capacity]
        seen = jnp.dot(tail, picks[k], preferred_element_type=F32)
        value = seen[0:1, :] + seen[1:2, :]
        total0 = total0 + jnp.where(first[k : k + 1, :], value, 0.0)
        total1 = total1 + jnp.where(second[k : k + 1, :], value, 0.0)
    comb = combine_ref[...].astype(F32)
    comb_ref[0:1, :] = total0 / comb[0:1, :]
    comb_ref[1:2, :] = total1 / comb[1:2, :]


def crossed(value, flips):
    experts, slots = lax.axis_size("expert"), lax.axis_size("dp")
    pairs = [
        (e * slots + d, (e ^ flips[d % 2]) * slots + d)
        for e in range(experts)
        for d in range(slots)
    ]
    return lax.ppermute(value, ("expert", "dp"), pairs)


def moved(value, message, back=False):
    shift, flip = message
    size = lax.axis_size("dp")
    chips = size // 2
    pairs = [(i, chip_after(i // 2, shift, chips) * 2 + (i % 2 ^ flip)) for i in range(size)]
    if back:
        pairs = sorted((b, a) for a, b in pairs)
    return lax.ppermute(value, "dp", pairs)


def vmem(mib):
    return pltpu.CompilerParams(vmem_limit_bytes=mib * 1024 * 1024)


def shape_of(*dims, dtype=BF16):
    return jax.ShapeDtypeStruct(dims, dtype)


def in_hbm(count):
    return [pl.BlockSpec(memory_space=HBM)] * count


def in_vmem(count):
    return [pl.BlockSpec(memory_space=pltpu.MemorySpace.VMEM)] * count


def kept_in_hbm(value):
    return pltpu.with_memory_space_constraint(value, HBM)


def anywhere(count):
    return [pl.BlockSpec(memory_space=pl.ANY)] * count


def run_hold(*weights):
    return pl.pallas_call(
        hold_kernel,
        in_specs=in_hbm(len(weights)),
        out_specs=in_vmem(len(weights)),
        out_shape=[shape_of(*value.shape) for value in weights],
        scratch_shapes=[pltpu.SemaphoreType.DMA((len(weights),))],
        compiler_params=vmem(16),
        cost_estimate=NO_COST,
    )(*map(kept_in_hbm, weights))


def run_relay(whole, *earlier):
    rows, width = whole.shape[0] // 2, whole.shape[1]
    return pl.pallas_call(
        functools.partial(relay_kernel, rows),
        in_specs=in_vmem(1) + anywhere(len(earlier)),
        out_specs=in_vmem(1)[0],
        out_shape=shape_of(rows, width),
        compiler_params=vmem(16),
        cost_estimate=NO_COST,
    )(whole, *earlier)


def run_forward(blocks, capacity, weights, *earlier):
    count = len(blocks)
    _, width, hidden = weights[0].shape
    return pl.pallas_call(
        functools.partial(forward_kernel, count, capacity, 256),
        in_specs=in_vmem(count + 3) + anywhere(len(earlier)),
        out_specs=in_vmem(1)[0],
        out_shape=shape_of(3, count * capacity, hidden),
        compiler_params=vmem(24),
        cost_estimate=NO_COST,
    )(*blocks, *weights, *earlier)


def run_backward(sums, count, capacity, w_gate, w_up, *earlier):
    _, width, hidden = w_gate.shape
    rows = count * capacity
    length = width // LANES * capacity + 16
    return pl.pallas_call(
        functools.partial(backward_kernel, count, capacity, 256),
        in_specs=in_vmem(4) + anywhere(len(earlier)),
        out_specs=in_vmem(3 + count),
        out_shape=[shape_of(rows, hidden)] * 3 + [shape_of(length, LANES)] * count,
        compiler_params=vmem(24),
        cost_estimate=NO_COST,
    )(*sums, w_gate, w_up, *earlier)


def run_weights(blocks, capacity, kept, hidden, *earlier):
    count, chunks = len(blocks), len(kept)
    width = blocks[0].shape[1]
    tile = 256
    column = pl.BlockSpec((2 * capacity, tile), lambda j: (0, j))
    flat = [kept[c][i] for i in range(3) for c in range(chunks)]
    held = [pl.BlockSpec(value.shape, lambda j: (0, 0)) for value in flat]
    row = pl.BlockSpec((1, tile, hidden), lambda j: (0, j, 0))
    return pl.pallas_call(
        functools.partial(weight_kernel, count, capacity, chunks),
        grid=(width // tile,),
        in_specs=[column] * count + held + anywhere(len(earlier)),
        out_specs=[row, row, pl.BlockSpec((1, hidden, tile), lambda j: (0, 0, j))],
        out_shape=[shape_of(1, width, hidden)] * 2 + [shape_of(1, hidden, width)],
        compiler_params=vmem(40),
        cost_estimate=NO_COST,
    )(*blocks, *flat, *earlier)


def expert_total(part, *earlier):
    got = crossed(part, (1, 2))
    if earlier:
        got = lax.optimization_barrier((got, *earlier))[0]
    pair = (part.astype(F32) + got.astype(F32)).astype(BF16)
    return pair, crossed(pair, (2, 1))


SHIFTS = (0, 3, 1, 2)
MESSAGES = tuple((shift, flip) for shift in SHIFTS for flip in (0, 1))


def after(value, *others):
    return lax.optimization_barrier((value, *others))[0]


def exchange_body(tokens, routes, combine, cotangent, w_gate, w_up, w_down):
    tok_rows, width = tokens.shape
    top_routes = routes.shape[1]
    experts = lax.axis_size("dp")
    capacity = 3 * tok_rows * top_routes // (2 * experts)
    hidden = w_gate.shape[2]
    routes_t, combine_t = routes.T, combine.T
    chunks = len(SHIFTS)
    sends = pl.pallas_call(
        functools.partial(send_kernel, MESSAGES, capacity, experts),
        in_specs=in_hbm(4),
        out_specs=in_vmem(chunks + 1),
        out_shape=[shape_of(2 * capacity, width)] * 2
        + [shape_of(4 * capacity, width)] * (chunks - 1),
        scratch_shapes=[
            pltpu.VMEM(routes_t.shape, jnp.int32),
            pltpu.VMEM(combine_t.shape, BF16),
            pltpu.VMEM(tokens.shape, BF16),
            pltpu.VMEM(tokens.shape, BF16),
            pltpu.SemaphoreType.DMA((4,)),
        ],
        compiler_params=vmem(32),
        cost_estimate=NO_COST,
    )(*map(kept_in_hbm, (routes_t, combine_t, tokens, cotangent)))
    weights = run_hold(w_gate, w_up, w_down)
    wholes = [sends[0]]
    for shift, value in zip(SHIFTS[1:], sends[2:]):
        wholes.append(moved(value, (shift, 0)))
    blocks, parts, sums, kept, backs = [], [], [], [], []

    def receive(i, *earlier):
        other = run_relay(wholes[i], *earlier) if i else sends[1]
        blocks.append((wholes[i], moved(other, (0, 1))))

    def forward(i, *earlier):
        parts.append(run_forward(blocks[i], capacity, weights, *earlier))

    def exchange(i, *earlier):
        sums.append(expert_total(parts[i], *earlier))

    def backward(i, *earlier):
        out = run_backward(sums[i], 2, capacity, *weights[:2], *earlier)
        kept.append(out[:3])
        for message, value in zip(MESSAGES[2 * i : 2 * i + 2], out[3:]):
            backs.append(value if message == (0, 0) else moved(value, message, back=True))

    receive(0)
    receive(1)
    receive(2)
    forward(0)
    exchange(0)
    forward(1, sums[0][0])
    exchange(1)
    backward(0, parts[1])
    forward(2, sums[1][0], kept[0][0])
    exchange(2)
    backward(1, parts[2])
    receive(3, kept[1][0])
    forward(3, sums[2][0], kept[1][0])
    backward(2, parts[3])
    exchange(3, *backs[2:4], kept[2][0])
    backward(3, kept[2][0])
    flat = [block for pair in blocks for block in pair]
    grad_gate, grad_up, grad_down = run_weights(flat, capacity, kept, hidden)
    token_grad, comb_grad = pl.pallas_call(
        functools.partial(merge_kernel, MESSAGES, capacity, experts, 0),
        in_specs=in_vmem(2 + experts),
        out_specs=in_vmem(2),
        out_shape=[shape_of(tok_rows, width), shape_of(top_routes, tok_rows, dtype=F32)],
        compiler_params=vmem(32),
        cost_estimate=NO_COST,
    )(routes_t, combine_t, *backs)
    return (token_grad, comb_grad.T, grad_gate, grad_up, grad_down)


def gather_body(tokens, routes, combine, cotangent, w_gate, w_up, w_down):
    tok_rows, slice_width = tokens.shape
    top_routes = routes.shape[1]
    experts = lax.axis_size("dp")
    capacity = 3 * tok_rows * top_routes // (2 * experts)
    route_count = tok_rows * top_routes
    slot_total = experts * capacity
    route_flat = routes.reshape(route_count)
    onehot = (route_flat[:, None] == jnp.arange(experts, dtype=jnp.int32)[None, :]).astype(
        jnp.int32
    )
    slot_rank = jnp.sum((jnp.cumsum(onehot, axis=0) - onehot) * onehot, axis=1)
    places = route_flat * capacity + slot_rank
    source = jnp.full((slot_total,), route_count, jnp.int32)
    source = source.at[places].set(jnp.arange(route_count, dtype=jnp.int32))
    blank_row = jnp.zeros((1, slice_width), BF16)
    token_send = jnp.concatenate([tokens, blank_row], axis=0)[source // top_routes]
    cot_send = jnp.concatenate([cotangent, blank_row], axis=0)[source // top_routes]
    comb_send = jnp.concatenate(
        [combine.reshape(route_count), jnp.zeros((1,), BF16)], axis=0
    )[source]
    spread = functools.partial(
        lax.all_to_all, axis_name="dp", split_axis=0, concat_axis=0, tiled=True
    )
    token_slots = spread(token_send.reshape(experts, capacity, slice_width)).reshape(
        slot_total, slice_width
    )
    cot_slots = spread(cot_send.reshape(experts, capacity, slice_width)).reshape(
        slot_total, slice_width
    )
    comb_slots = spread(comb_send.reshape(experts, capacity)).reshape(slot_total).astype(F32)
    gate_mat, up_mat, down_mat = w_gate[0], w_up[0], w_down[0]
    partials = jnp.stack(
        [
            jnp.dot(token_slots, gate_mat, preferred_element_type=F32),
            jnp.dot(token_slots, up_mat, preferred_element_type=F32),
            contract_last(cot_slots, down_mat),
        ],
        axis=1,
    )
    summed = lax.psum_scatter(
        partials.astype(BF16), "expert", scatter_dimension=2, tiled=True
    ).astype(F32)
    hidden_part, gate_part, up_part = swiglu_grads(
        summed[:, 0], summed[:, 1], summed[:, 2], comb_slots
    )
    slot_comb = jnp.sum(hidden_part.astype(F32) * summed[:, 2], axis=1)
    joined = lax.all_gather(
        jnp.stack([hidden_part, gate_part, up_part], axis=1), "expert", axis=2, tiled=True
    )
    hidden, grad_gate_pre, grad_up_pre = joined[:, 0], joined[:, 1], joined[:, 2]
    slot_dx = contract_last(grad_gate_pre, gate_mat) + contract_last(grad_up_pre, up_mat)
    scaled_dy = (comb_slots[:, None] * cot_slots.astype(F32)).astype(BF16)
    grad_gate = contract_first(token_slots, grad_gate_pre).astype(BF16)[None]
    grad_up = contract_first(token_slots, grad_up_pre).astype(BF16)[None]
    grad_down = contract_first(hidden, scaled_dy).astype(BF16)[None]
    back_dx = spread(slot_dx.reshape(experts, capacity, slice_width).astype(BF16)).astype(F32)
    back_comb = spread(slot_comb.reshape(experts, capacity).astype(BF16)).astype(F32)
    route_dx = back_dx.reshape(slot_total, slice_width)[places].reshape(
        tok_rows, top_routes, slice_width
    )
    token_grad = jnp.sum(route_dx, axis=1).astype(BF16)
    comb_part = back_comb.reshape(slot_total)[places].reshape(tok_rows, top_routes)
    combine_grad = lax.psum(comb_part, "expert")
    return (token_grad, combine_grad, grad_gate, grad_up, grad_down)


def body(tokens, routes, combine, cotangent, w_gate, w_up, w_down):
    tok_rows, width = tokens.shape
    experts = lax.axis_size("dp")
    capacity = 3 * tok_rows * routes.shape[1] // (2 * experts)
    fits = (
        experts == 8
        and lax.axis_size("expert") == 4
        and routes.shape[1] == 2
        and tok_rows == LANES
        and capacity % 16 == 0
        and width % 256 == 0
        and w_gate.shape[2] % 256 == 0
    )
    run = exchange_body if fits else gather_body
    return run(tokens, routes, combine, cotangent, w_gate, w_up, w_down)


def solution(mesh):
    in_specs = (
        P("dp", "expert"),
        P("dp", None),
        P("dp", None),
        P("dp", "expert"),
        P("dp", "expert", None),
        P("dp", "expert", None),
        P("dp", None, "expert"),
    )
    out_specs = (
        P("dp", "expert"),
        P("dp", None),
        P("dp", "expert", None),
        P("dp", "expert", None),
        P("dp", None, "expert"),
    )
    return jax.shard_map(body, mesh=mesh, in_specs=in_specs, out_specs=out_specs, check_vma=False)
```

```python
import functools
import jax
import jax.numpy as jnp
from jax import lax
from jax.experimental import pallas as pl
from jax.experimental.pallas import tpu as pltpu
from jax.sharding import PartitionSpec as P

F32 = jnp.float32
BF16 = jnp.bfloat16
LANES = 128
NO_COST = pl.CostEstimate(flops=1, bytes_accessed=1, transcendentals=0)


def contract_last(matrix_a, matrix_b):
    return lax.dot_general(
        matrix_a, matrix_b, (((1,), (1,)), ((), ())), preferred_element_type=F32
    )


def contract_first(matrix_a, matrix_b):
    return lax.dot_general(
        matrix_a, matrix_b, (((0,), (0,)), ((), ())), preferred_element_type=F32
    )


def swiglu_grads(pre_gate, pre_up, back_hidden, weights):
    sigmas = jax.nn.sigmoid(pre_gate)
    active = pre_gate * sigmas
    hidden = (active * pre_up).astype(BF16)
    scaled = weights[:, None] * back_hidden
    grad_gate_pre = (scaled * pre_up * sigmas * (1.0 + pre_gate * (1.0 - sigmas))).astype(BF16)
    grad_up_pre = (scaled * active).astype(BF16)
    return (hidden, grad_gate_pre, grad_up_pre)


HBM = pltpu.MemorySpace.HBM


def chip_after(chip, shift, chips):
    place = (chip ^ (chip >> 1)) + shift & chips - 1
    return place ^ (place >> 1)


def slot_masks(routes, messages, capacity, experts):
    me = lax.axis_index("dp")
    tok_rows = routes.shape[1]
    row = lax.broadcasted_iota(jnp.int32, (len(messages), tok_rows), 0)
    expert = jnp.zeros((len(messages), tok_rows), jnp.int32)
    for k, (shift, flip) in enumerate(messages):
        target = chip_after(me // 2, shift, experts // 2) * 2 + jnp.bitwise_xor(me % 2, flip)
        expert = jnp.where(row == k, target, expert)
    first = routes[0:1, :] == expert
    second = routes[1:2, :] == expert
    named = jnp.where(first, 1.0, 0.0) + jnp.where(second, 1.0, 0.0)
    before = jnp.where(
        lax.broadcasted_iota(jnp.int32, (tok_rows, tok_rows), 0)
        < lax.broadcasted_iota(jnp.int32, (tok_rows, tok_rows), 1),
        1.0,
        0.0,
    ).astype(BF16)
    rank = jnp.dot(named.astype(BF16), before, preferred_element_type=F32).astype(jnp.int32)
    rank = jnp.where(named > 0.5, rank, -1)
    place = lax.broadcasted_iota(jnp.int32, (capacity, tok_rows), 0)
    hits = [place == rank[k : k + 1, :] for k in range(len(messages))]
    return first, second, hits


def send_kernel(messages, capacity, experts, routes_hbm, combine_hbm, tokens_hbm, cot_hbm, *refs):
    out_refs = refs[:-5]
    routes_ref, combine_ref, tokens_ref, cot_ref, sems = refs[-5:]
    pairs = (
        (routes_hbm, routes_ref),
        (combine_hbm, combine_ref),
        (tokens_hbm, tokens_ref),
        (cot_hbm, cot_ref),
    )
    copies = [pltpu.make_async_copy(a, b, sems.at[i]) for i, (a, b) in enumerate(pairs)]
    for copy in copies:
        copy.start()
    copies[0].wait()
    copies[1].wait()
    first, second, hits = slot_masks(routes_ref[...], messages, capacity, experts)
    comb = combine_ref[...].astype(F32)
    scale = jnp.where(first, comb[0:1, :], 0.0) + jnp.where(second, comb[1:2, :], 0.0)
    copies[2].wait()
    copies[3].wait()
    tokens = tokens_ref[...]
    cot = cot_ref[...]
    places = [(out, at) for out in out_refs for at in range(0, out.shape[0], 2 * capacity)]
    ones = [jnp.where(hit, 1.0, 0.0) for hit in hits]
    pick = jnp.concatenate(ones, axis=0).astype(BF16)
    weigh = jnp.concatenate([one * scale[k : k + 1, :] for k, one in enumerate(ones)], axis=0)
    picked = jnp.dot(pick, tokens, preferred_element_type=F32).astype(BF16)
    weighed = jnp.dot(weigh.astype(BF16), cot, preferred_element_type=F32).astype(BF16)
    for k, (out, at) in enumerate(places):
        rows = slice(k * capacity, (k + 1) * capacity)
        out[at : at + capacity, :] = picked[rows]
        out[at + capacity : at + 2 * capacity, :] = weighed[rows]


def hold_kernel(*refs):
    sems = refs[-1]
    count = len(refs) // 2
    copies = [
        pltpu.make_async_copy(refs[i], refs[count + i], sems.at[i]) for i in range(count)
    ]
    for copy in copies:
        copy.start()
    for copy in copies:
        copy.wait()


def relay_kernel(rows, whole_ref, *refs):
    refs[-1][...] = whole_ref[rows:, :]


def forward_kernel(blocks, capacity, tile, *refs):
    block_refs = refs[:blocks]
    weights = refs[blocks : blocks + 3]
    out_ref = refs[-1]
    tok = jnp.concatenate([ref[0:capacity, :] for ref in block_refs], axis=0)
    cot = jnp.concatenate([ref[capacity : 2 * capacity, :] for ref in block_refs], axis=0)

    def step(j, _):
        at = pl.ds(pl.multiple_of(j * tile, tile), tile)
        for i in range(3):
            if i < 2:
                part = jnp.dot(tok, weights[i][0, :, at], preferred_element_type=F32)
            else:
                part = contract_last(cot, weights[i][0, at, :])
            out_ref[i, :, at] = part.astype(BF16)
        return 0

    lax.fori_loop(0, out_ref.shape[2] // tile, step, 0, unroll=True)


def backward_kernel(blocks, capacity, tile, own_ref, got_ref, gate_ref, up_ref, *refs):
    out_refs = refs[-3 - blocks :]
    hid_ref, gg_ref, gu_ref = out_refs[:3]
    back_refs = out_refs[3:]
    width = gate_ref.shape[1]
    eye = lax.broadcasted_iota(jnp.int32, (capacity, LANES), 0) == lax.broadcasted_iota(
        jnp.int32, (capacity, LANES), 1
    )
    base = width // LANES * capacity
    for k in range(blocks):
        rows = slice(k * capacity, (k + 1) * capacity)
        pre_gate, pre_up, back_hidden = (
            own_ref[i, rows, :].astype(F32) + got_ref[i, rows, :].astype(F32) for i in range(3)
        )
        sigmas = jax.nn.sigmoid(pre_gate)
        active = pre_gate * sigmas
        hidden = (active * pre_up).astype(BF16)
        gg = back_hidden * pre_up * sigmas * (1.0 + pre_gate * (1.0 - sigmas))
        hid_ref[rows, :] = hidden
        gg_ref[rows, :] = gg.astype(BF16)
        gu_ref[rows, :] = (back_hidden * active).astype(BF16)
        comb = jnp.sum(hidden.astype(F32) * back_hidden, axis=1, keepdims=True)
        row = jnp.sum(jnp.where(eye, comb, 0.0), axis=0, keepdims=True)
        high = row.astype(BF16)
        low = (row - high.astype(F32)).astype(BF16)
        tail = jnp.concatenate(
            [high.astype(F32), low.astype(F32), jnp.zeros((14, LANES), F32)], axis=0
        )
        back_refs[k][base : base + 16, :] = tail.astype(BF16)
    gg, gu = gg_ref[...], gu_ref[...]
    per = tile // LANES

    def step(j, _):
        at = pl.ds(pl.multiple_of(j * tile, tile), tile)
        dx = contract_last(gg, gate_ref[0, at, :]) + contract_last(gu, up_ref[0, at, :])
        dx = dx.astype(BF16)
        start = pl.multiple_of(j * (per * capacity), per * capacity)
        for k in range(blocks):
            part = dx[k * capacity : (k + 1) * capacity, :]
            stacked = jnp.concatenate(
                [part[:, c * LANES : (c + 1) * LANES] for c in range(per)], axis=0
            )
            back_refs[k][pl.ds(start, per * capacity), :] = stacked
        return 0

    lax.fori_loop(0, width // tile, step, 0, unroll=True)


def weight_kernel(blocks, capacity, chunks, *refs):
    block_refs = refs[:blocks]
    hid_refs = refs[blocks : blocks + chunks]
    gg_refs = refs[blocks + chunks : blocks + 2 * chunks]
    gu_refs = refs[blocks + 2 * chunks : blocks + 3 * chunks]
    gate_ref, up_ref, down_ref = refs[-3:]
    tok = jnp.concatenate([ref[0:capacity, :] for ref in block_refs], axis=0)
    cot = jnp.concatenate([ref[capacity : 2 * capacity, :] for ref in block_refs], axis=0)
    join = lambda part: jnp.concatenate([ref[...] for ref in part], axis=0)
    gate_ref[0] = contract_first(tok, join(gg_refs)).astype(BF16)
    up_ref[0] = contract_first(tok, join(gu_refs)).astype(BF16)
    down_ref[0] = contract_first(join(hid_refs), cot).astype(BF16)


def merge_kernel(messages, capacity, experts, early, *refs):
    routes_ref, combine_ref = refs[early : early + 2]
    back_refs = refs[early + 2 : -2]
    grad_ref, comb_ref = refs[-2:]
    first, second, hits = slot_masks(routes_ref[...], messages, capacity, experts)
    picks = [jnp.where(hit, 1.0, 0.0).astype(BF16) for hit in hits]
    ones = [jnp.where(hit, 1.0, 0.0) for hit in hits]
    pick = jnp.concatenate(ones, axis=0).T.astype(BF16)
    groups = grad_ref.shape[1] // LANES
    for c in range(0, groups, 2):
        pieces = [
            jnp.concatenate([ref[b * capacity : (b + 1) * capacity, :] for ref in back_refs], axis=0)
            for b in (c, c + 1)
        ]
        piece = jnp.concatenate(pieces, axis=1)
        total = jnp.dot(pick, piece, preferred_element_type=F32)
        grad_ref[:, c * LANES : (c + 2) * LANES] = total.astype(BF16)
    total0 = jnp.zeros((1, LANES), F32)
    total1 = total0
    for k in range(len(messages)):
        tail = back_refs[k][groups * capacity : groups * capacity + 16, :][:, :capacity]
        seen = jnp.dot(tail, picks[k], preferred_element_type=F32)
        value = seen[0:1, :] + seen[1:2, :]
        total0 = total0 + jnp.where(first[k : k + 1, :], value, 0.0)
        total1 = total1 + jnp.where(second[k : k + 1, :], value, 0.0)
    comb = combine_ref[...].astype(F32)
    comb_ref[0:1, :] = total0 / comb[0:1, :]
    comb_ref[1:2, :] = total1 / comb[1:2, :]


def crossed(value, flips):
    experts, slots = lax.axis_size("expert"), lax.axis_size("dp")
    pairs = [
        (e * slots + d, (e ^ flips[d % 2]) * slots + d)
        for e in range(experts)
        for d in range(slots)
    ]
    return lax.ppermute(value, ("expert", "dp"), pairs)


def moved(value, message, back=False):
    shift, flip = message
    size = lax.axis_size("dp")
    chips = size // 2
    pairs = [(i, chip_after(i // 2, shift, chips) * 2 + (i % 2 ^ flip)) for i in range(size)]
    if back:
        pairs = sorted((b, a) for a, b in pairs)
    return lax.ppermute(value, "dp", pairs)


def vmem(mib):
    return pltpu.CompilerParams(vmem_limit_bytes=mib * 1024 * 1024)


def shape_of(*dims, dtype=BF16):
    return jax.ShapeDtypeStruct(dims, dtype)


def in_hbm(count):
    return [pl.BlockSpec(memory_space=HBM)] * count


def in_vmem(count):
    return [pl.BlockSpec(memory_space=pltpu.MemorySpace.VMEM)] * count


def kept_in_hbm(value):
    return pltpu.with_memory_space_constraint(value, HBM)


def anywhere(count):
    return [pl.BlockSpec(memory_space=pl.ANY)] * count


def run_hold(*weights):
    return pl.pallas_call(
        hold_kernel,
        in_specs=in_hbm(len(weights)),
        out_specs=in_vmem(len(weights)),
        out_shape=[shape_of(*value.shape) for value in weights],
        scratch_shapes=[pltpu.SemaphoreType.DMA((len(weights),))],
        compiler_params=vmem(16),
        cost_estimate=NO_COST,
    )(*map(kept_in_hbm, weights))


def run_relay(whole, *earlier):
    rows, width = whole.shape[0] // 2, whole.shape[1]
    return pl.pallas_call(
        functools.partial(relay_kernel, rows),
        in_specs=in_vmem(1) + anywhere(len(earlier)),
        out_specs=in_vmem(1)[0],
        out_shape=shape_of(rows, width),
        compiler_params=vmem(16),
        cost_estimate=NO_COST,
    )(whole, *earlier)


def run_forward(blocks, capacity, weights, *earlier):
    count = len(blocks)
    _, width, hidden = weights[0].shape
    return pl.pallas_call(
        functools.partial(forward_kernel, count, capacity, 256),
        in_specs=in_vmem(count + 3) + anywhere(len(earlier)),
        out_specs=in_vmem(1)[0],
        out_shape=shape_of(3, count * capacity, hidden),
        compiler_params=vmem(24),
        cost_estimate=NO_COST,
    )(*blocks, *weights, *earlier)


def run_backward(sums, count, capacity, w_gate, w_up, *earlier):
    _, width, hidden = w_gate.shape
    rows = count * capacity
    length = width // LANES * capacity + 16
    return pl.pallas_call(
        functools.partial(backward_kernel, count, capacity, 256),
        in_specs=in_vmem(4) + anywhere(len(earlier)),
        out_specs=in_vmem(3 + count),
        out_shape=[shape_of(rows, hidden)] * 3 + [shape_of(length, LANES)] * count,
        compiler_params=vmem(24),
        cost_estimate=NO_COST,
    )(*sums, w_gate, w_up, *earlier)


def run_weights(blocks, capacity, kept, hidden, *earlier):
    count, chunks = len(blocks), len(kept)
    width = blocks[0].shape[1]
    tile = 256
    column = pl.BlockSpec((2 * capacity, tile), lambda j: (0, j))
    flat = [kept[c][i] for i in range(3) for c in range(chunks)]
    held = [pl.BlockSpec(value.shape, lambda j: (0, 0)) for value in flat]
    row = pl.BlockSpec((1, tile, hidden), lambda j: (0, j, 0))
    return pl.pallas_call(
        functools.partial(weight_kernel, count, capacity, chunks),
        grid=(width // tile,),
        in_specs=[column] * count + held + anywhere(len(earlier)),
        out_specs=[row, row, pl.BlockSpec((1, hidden, tile), lambda j: (0, 0, j))],
        out_shape=[shape_of(1, width, hidden)] * 2 + [shape_of(1, hidden, width)],
        compiler_params=vmem(40),
        cost_estimate=NO_COST,
    )(*blocks, *flat, *earlier)


def expert_total(part, *earlier):
    got = crossed(part, (1, 2))
    if earlier:
        got = lax.optimization_barrier((got, *earlier))[0]
    pair = (part.astype(F32) + got.astype(F32)).astype(BF16)
    return pair, crossed(pair, (2, 1))


SHIFTS = (0, 3, 1, 2)
MESSAGES = tuple((shift, flip) for shift in SHIFTS for flip in (0, 1))


def after(value, *others):
    return lax.optimization_barrier((value, *others))[0]


def exchange_body(tokens, routes, combine, cotangent, w_gate, w_up, w_down):
    tok_rows, width = tokens.shape
    top_routes = routes.shape[1]
    experts = lax.axis_size("dp")
    capacity = 3 * tok_rows * top_routes // (2 * experts)
    hidden = w_gate.shape[2]
    routes_t, combine_t = routes.T, combine.T
    chunks = len(SHIFTS)
    sends = pl.pallas_call(
        functools.partial(send_kernel, MESSAGES, capacity, experts),
        in_specs=in_hbm(4),
        out_specs=in_vmem(chunks + 1),
        out_shape=[shape_of(2 * capacity, width)] * 2
        + [shape_of(4 * capacity, width)] * (chunks - 1),
        scratch_shapes=[
            pltpu.VMEM(routes_t.shape, jnp.int32),
            pltpu.VMEM(combine_t.shape, BF16),
            pltpu.VMEM(tokens.shape, BF16),
            pltpu.VMEM(tokens.shape, BF16),
            pltpu.SemaphoreType.DMA((4,)),
        ],
        compiler_params=vmem(32),
        cost_estimate=NO_COST,
    )(*map(kept_in_hbm, (routes_t, combine_t, tokens, cotangent)))
    weights = run_hold(w_gate, w_up, w_down)
    wholes = [sends[0]]
    for shift, value in zip(SHIFTS[1:], sends[2:]):
        wholes.append(moved(value, (shift, 0)))
    blocks, parts, sums, kept, backs = [], [], [], [], []

    def receive(i, *earlier):
        other = run_relay(wholes[i], *earlier) if i else sends[1]
        blocks.append((wholes[i], moved(other, (0, 1))))

    def forward(i, *earlier):
        parts.append(run_forward(blocks[i], capacity, weights, *earlier))

    def exchange(i, *earlier):
        sums.append(expert_total(parts[i], *earlier))

    def backward(i, *earlier):
        out = run_backward(sums[i], 2, capacity, *weights[:2], *earlier)
        kept.append(out[:3])
        for message, value in zip(MESSAGES[2 * i : 2 * i + 2], out[3:]):
            backs.append(value if message == (0, 0) else moved(value, message, back=True))

    receive(0)
    receive(1)
    receive(2)
    forward(0)
    exchange(0)
    forward(1, sums[0][0])
    exchange(1)
    backward(0, parts[1])
    forward(2, sums[1][0], kept[0][0])
    exchange(2)
    backward(1, parts[2])
    receive(3, kept[1][0])
    forward(3, sums[2][0], kept[1][0])
    backward(2, parts[3])
    exchange(3, *backs[2:4], kept[2][0])
    backward(3, kept[2][0])
    flat = [block for pair in blocks for block in pair]
    grad_gate, grad_up, grad_down = run_weights(flat, capacity, kept, hidden)
    token_grad, comb_grad = pl.pallas_call(
        functools.partial(merge_kernel, MESSAGES, capacity, experts, 0),
        in_specs=in_vmem(2 + experts),
        out_specs=in_vmem(2),
        out_shape=[shape_of(tok_rows, width), shape_of(top_routes, tok_rows, dtype=F32)],
        compiler_params=vmem(32),
        cost_estimate=NO_COST,
    )(routes_t, combine_t, *backs)
    return (token_grad, comb_grad.T, grad_gate, grad_up, grad_down)


def gather_body(tokens, routes, combine, cotangent, w_gate, w_up, w_down):
    tok_rows, slice_width = tokens.shape
    top_routes = routes.shape[1]
    experts = lax.axis_size("dp")
    capacity = 3 * tok_rows * top_routes // (2 * experts)
    route_count = tok_rows * top_routes
    slot_total = experts * capacity
    route_flat = routes.reshape(route_count)
    onehot = (route_flat[:, None] == jnp.arange(experts, dtype=jnp.int32)[None, :]).astype(
        jnp.int32
    )
    slot_rank = jnp.sum((jnp.cumsum(onehot, axis=0) - onehot) * onehot, axis=1)
    places = route_flat * capacity + slot_rank
    source = jnp.full((slot_total,), route_count, jnp.int32)
    source = source.at[places].set(jnp.arange(route_count, dtype=jnp.int32))
    blank_row = jnp.zeros((1, slice_width), BF16)
    token_send = jnp.concatenate([tokens, blank_row], axis=0)[source // top_routes]
    cot_send = jnp.concatenate([cotangent, blank_row], axis=0)[source // top_routes]
    comb_send = jnp.concatenate(
        [combine.reshape(route_count), jnp.zeros((1,), BF16)], axis=0
    )[source]
    spread = functools.partial(
        lax.all_to_all, axis_name="dp", split_axis=0, concat_axis=0, tiled=True
    )
    token_slots = spread(token_send.reshape(experts, capacity, slice_width)).reshape(
        slot_total, slice_width
    )
    cot_slots = spread(cot_send.reshape(experts, capacity, slice_width)).reshape(
        slot_total, slice_width
    )
    comb_slots = spread(comb_send.reshape(experts, capacity)).reshape(slot_total).astype(F32)
    gate_mat, up_mat, down_mat = w_gate[0], w_up[0], w_down[0]
    partials = jnp.stack(
        [
            jnp.dot(token_slots, gate_mat, preferred_element_type=F32),
            jnp.dot(token_slots, up_mat, preferred_element_type=F32),
            contract_last(cot_slots, down_mat),
        ],
        axis=1,
    )
    summed = lax.psum_scatter(
        partials.astype(BF16), "expert", scatter_dimension=2, tiled=True
    ).astype(F32)
    hidden_part, gate_part, up_part = swiglu_grads(
        summed[:, 0], summed[:, 1], summed[:, 2], comb_slots
    )
    slot_comb = jnp.sum(hidden_part.astype(F32) * summed[:, 2], axis=1)
    joined = lax.all_gather(
        jnp.stack([hidden_part, gate_part, up_part], axis=1), "expert", axis=2, tiled=True
    )
    hidden, grad_gate_pre, grad_up_pre = joined[:, 0], joined[:, 1], joined[:, 2]
    slot_dx = contract_last(grad_gate_pre, gate_mat) + contract_last(grad_up_pre, up_mat)
    scaled_dy = (comb_slots[:, None] * cot_slots.astype(F32)).astype(BF16)
    grad_gate = contract_first(token_slots, grad_gate_pre).astype(BF16)[None]
    grad_up = contract_first(token_slots, grad_up_pre).astype(BF16)[None]
    grad_down = contract_first(hidden, scaled_dy).astype(BF16)[None]
    back_dx = spread(slot_dx.reshape(experts, capacity, slice_width).astype(BF16)).astype(F32)
    back_comb = spread(slot_comb.reshape(experts, capacity).astype(BF16)).astype(F32)
    route_dx = back_dx.reshape(slot_total, slice_width)[places].reshape(
        tok_rows, top_routes, slice_width
    )
    token_grad = jnp.sum(route_dx, axis=1).astype(BF16)
    comb_part = back_comb.reshape(slot_total)[places].reshape(tok_rows, top_routes)
    combine_grad = lax.psum(comb_part, "expert")
    return (token_grad, combine_grad, grad_gate, grad_up, grad_down)


def body(tokens, routes, combine, cotangent, w_gate, w_up, w_down):
    tok_rows, width = tokens.shape
    experts = lax.axis_size("dp")
    capacity = 3 * tok_rows * routes.shape[1] // (2 * experts)
    fits = (
        experts == 8
        and lax.axis_size("expert") == 4
        and routes.shape[1] == 2
        and tok_rows == LANES
        and capacity % 16 == 0
        and width % 256 == 0
        and w_gate.shape[2] % 256 == 0
    )
    run = exchange_body if fits else gather_body
    return run(tokens, routes, combine, cotangent, w_gate, w_up, w_down)


def solution(mesh):
    in_specs = (
        P("dp", "expert"),
        P("dp", None),
        P("dp", None),
        P("dp", "expert"),
        P("dp", "expert", None),
        P("dp", "expert", None),
        P("dp", None, "expert"),
    )
    out_specs = (
        P("dp", "expert"),
        P("dp", None),
        P("dp", "expert", None),
        P("dp", "expert", None),
        P("dp", None, "expert"),
    )
    return jax.shard_map(body, mesh=mesh, in_specs=in_specs, out_specs=out_specs, check_vma=False)
```

```python
import functools
import jax
import jax.numpy as jnp
from jax import lax
from jax.experimental import pallas as pl
from jax.experimental.pallas import tpu as pltpu
from jax.sharding import PartitionSpec as P

F32 = jnp.float32
BF16 = jnp.bfloat16
LANES = 128
NO_COST = pl.CostEstimate(flops=1, bytes_accessed=1, transcendentals=0)


def contract_last(matrix_a, matrix_b):
    return lax.dot_general(
        matrix_a, matrix_b, (((1,), (1,)), ((), ())), preferred_element_type=F32
    )


def contract_first(matrix_a, matrix_b):
    return lax.dot_general(
        matrix_a, matrix_b, (((0,), (0,)), ((), ())), preferred_element_type=F32
    )


def swiglu_grads(pre_gate, pre_up, back_hidden, weights):
    sigmas = jax.nn.sigmoid(pre_gate)
    active = pre_gate * sigmas
    hidden = (active * pre_up).astype(BF16)
    scaled = weights[:, None] * back_hidden
    grad_gate_pre = (scaled * pre_up * sigmas * (1.0 + pre_gate * (1.0 - sigmas))).astype(BF16)
    grad_up_pre = (scaled * active).astype(BF16)
    return (hidden, grad_gate_pre, grad_up_pre)


HBM = pltpu.MemorySpace.HBM


def chip_after(chip, shift, chips):
    place = (chip ^ (chip >> 1)) + shift & chips - 1
    return place ^ (place >> 1)


def slot_masks(routes, messages, capacity, experts):
    me = lax.axis_index("dp")
    tok_rows = routes.shape[1]
    row = lax.broadcasted_iota(jnp.int32, (len(messages), tok_rows), 0)
    expert = jnp.zeros((len(messages), tok_rows), jnp.int32)
    for k, (shift, flip) in enumerate(messages):
        target = chip_after(me // 2, shift, experts // 2) * 2 + jnp.bitwise_xor(me % 2, flip)
        expert = jnp.where(row == k, target, expert)
    first = routes[0:1, :] == expert
    second = routes[1:2, :] == expert
    named = jnp.where(first, 1.0, 0.0) + jnp.where(second, 1.0, 0.0)
    before = jnp.where(
        lax.broadcasted_iota(jnp.int32, (tok_rows, tok_rows), 0)
        < lax.broadcasted_iota(jnp.int32, (tok_rows, tok_rows), 1),
        1.0,
        0.0,
    ).astype(BF16)
    rank = jnp.dot(named.astype(BF16), before, preferred_element_type=F32).astype(jnp.int32)
    rank = jnp.where(named > 0.5, rank, -1)
    place = lax.broadcasted_iota(jnp.int32, (capacity, tok_rows), 0)
    hits = [place == rank[k : k + 1, :] for k in range(len(messages))]
    return first, second, hits


def send_kernel(messages, capacity, experts, routes_hbm, combine_hbm, tokens_hbm, cot_hbm, *refs):
    out_refs = refs[:-5]
    routes_ref, combine_ref, tokens_ref, cot_ref, sems = refs[-5:]
    pairs = (
        (routes_hbm, routes_ref),
        (combine_hbm, combine_ref),
        (tokens_hbm, tokens_ref),
        (cot_hbm, cot_ref),
    )
    copies = [pltpu.make_async_copy(a, b, sems.at[i]) for i, (a, b) in enumerate(pairs)]
    for copy in copies:
        copy.start()
    copies[0].wait()
    copies[1].wait()
    first, second, hits = slot_masks(routes_ref[...], messages, capacity, experts)
    comb = combine_ref[...].astype(F32)
    scale = jnp.where(first, comb[0:1, :], 0.0) + jnp.where(second, comb[1:2, :], 0.0)
    copies[2].wait()
    copies[3].wait()
    tokens = tokens_ref[...]
    cot = cot_ref[...]
    places = [(out, at) for out in out_refs for at in range(0, out.shape[0], 2 * capacity)]
    ones = [jnp.where(hit, 1.0, 0.0) for hit in hits]
    pick = jnp.concatenate(ones, axis=0).astype(BF16)
    weigh = jnp.concatenate([one * scale[k : k + 1, :] for k, one in enumerate(ones)], axis=0)
    picked = jnp.dot(pick, tokens, preferred_element_type=F32).astype(BF16)
    weighed = jnp.dot(weigh.astype(BF16), cot, preferred_element_type=F32).astype(BF16)
    for k, (out, at) in enumerate(places):
        rows = slice(k * capacity, (k + 1) * capacity)
        out[at : at + capacity, :] = picked[rows]
        out[at + capacity : at + 2 * capacity, :] = weighed[rows]


def hold_kernel(*refs):
    sems = refs[-1]
    count = len(refs) // 2
    copies = [
        pltpu.make_async_copy(refs[i], refs[count + i], sems.at[i]) for i in range(count)
    ]
    for copy in copies:
        copy.start()
    for copy in copies:
        copy.wait()


def relay_kernel(rows, whole_ref, *refs):
    refs[-1][...] = whole_ref[rows:, :]


def forward_kernel(blocks, capacity, tile, *refs):
    block_refs = refs[:blocks]
    weights = refs[blocks : blocks + 3]
    out_ref = refs[-1]
    tok = jnp.concatenate([ref[0:capacity, :] for ref in block_refs], axis=0)
    cot = jnp.concatenate([ref[capacity : 2 * capacity, :] for ref in block_refs], axis=0)

    def step(j, _):
        at = pl.ds(pl.multiple_of(j * tile, tile), tile)
        for i in range(3):
            if i < 2:
                part = jnp.dot(tok, weights[i][0, :, at], preferred_element_type=F32)
            else:
                part = contract_last(cot, weights[i][0, at, :])
            out_ref[i, :, at] = part.astype(BF16)
        return 0

    lax.fori_loop(0, out_ref.shape[2] // tile, step, 0, unroll=True)


def backward_kernel(blocks, capacity, tile, own_ref, got_ref, gate_ref, up_ref, *refs):
    out_refs = refs[-3 - blocks :]
    hid_ref, gg_ref, gu_ref = out_refs[:3]
    back_refs = out_refs[3:]
    width = gate_ref.shape[1]
    eye = lax.broadcasted_iota(jnp.int32, (capacity, LANES), 0) == lax.broadcasted_iota(
        jnp.int32, (capacity, LANES), 1
    )
    base = width // LANES * capacity
    for k in range(blocks):
        rows = slice(k * capacity, (k + 1) * capacity)
        pre_gate, pre_up, back_hidden = (
            own_ref[i, rows, :].astype(F32) + got_ref[i, rows, :].astype(F32) for i in range(3)
        )
        sigmas = jax.nn.sigmoid(pre_gate)
        active = pre_gate * sigmas
        hidden = (active * pre_up).astype(BF16)
        gg = back_hidden * pre_up * sigmas * (1.0 + pre_gate * (1.0 - sigmas))
        hid_ref[rows, :] = hidden
        gg_ref[rows, :] = gg.astype(BF16)
        gu_ref[rows, :] = (back_hidden * active).astype(BF16)
        comb = jnp.sum(hidden.astype(F32) * back_hidden, axis=1, keepdims=True)
        row = jnp.sum(jnp.where(eye, comb, 0.0), axis=0, keepdims=True)
        high = row.astype(BF16)
        low = (row - high.astype(F32)).astype(BF16)
        tail = jnp.concatenate(
            [high.astype(F32), low.astype(F32), jnp.zeros((14, LANES), F32)], axis=0
        )
        back_refs[k][base : base + 16, :] = tail.astype(BF16)
    gg, gu = gg_ref[...], gu_ref[...]
    per = tile // LANES

    def step(j, _):
        at = pl.ds(pl.multiple_of(j * tile, tile), tile)
        dx = contract_last(gg, gate_ref[0, at, :]) + contract_last(gu, up_ref[0, at, :])
        dx = dx.astype(BF16)
        start = pl.multiple_of(j * (per * capacity), per * capacity)
        for k in range(blocks):
            part = dx[k * capacity : (k + 1) * capacity, :]
            stacked = jnp.concatenate(
                [part[:, c * LANES : (c + 1) * LANES] for c in range(per)], axis=0
            )
            back_refs[k][pl.ds(start, per * capacity), :] = stacked
        return 0

    lax.fori_loop(0, width // tile, step, 0, unroll=True)


def weight_kernel(blocks, capacity, chunks, *refs):
    block_refs = refs[:blocks]
    hid_refs = refs[blocks : blocks + chunks]
    gg_refs = refs[blocks + chunks : blocks + 2 * chunks]
    gu_refs = refs[blocks + 2 * chunks : blocks + 3 * chunks]
    gate_ref, up_ref, down_ref = refs[-3:]
    tok = jnp.concatenate([ref[0:capacity, :] for ref in block_refs], axis=0)
    cot = jnp.concatenate([ref[capacity : 2 * capacity, :] for ref in block_refs], axis=0)
    join = lambda part: jnp.concatenate([ref[...] for ref in part], axis=0)
    gate_ref[0] = contract_first(tok, join(gg_refs)).astype(BF16)
    up_ref[0] = contract_first(tok, join(gu_refs)).astype(BF16)
    down_ref[0] = contract_first(join(hid_refs), cot).astype(BF16)


def merge_kernel(messages, capacity, experts, early, *refs):
    routes_ref, combine_ref = refs[early : early + 2]
    back_refs = refs[early + 2 : -2]
    grad_ref, comb_ref = refs[-2:]
    first, second, hits = slot_masks(routes_ref[...], messages, capacity, experts)
    picks = [jnp.where(hit, 1.0, 0.0).astype(BF16) for hit in hits]
    ones = [jnp.where(hit, 1.0, 0.0) for hit in hits]
    pick = jnp.concatenate(ones, axis=0).T.astype(BF16)
    groups = grad_ref.shape[1] // LANES
    for c in range(0, groups, 2):
        pieces = [
            jnp.concatenate([ref[b * capacity : (b + 1) * capacity, :] for ref in back_refs], axis=0)
            for b in (c, c + 1)
        ]
        piece = jnp.concatenate(pieces, axis=1)
        total = jnp.dot(pick, piece, preferred_element_type=F32)
        grad_ref[:, c * LANES : (c + 2) * LANES] = total.astype(BF16)
    total0 = jnp.zeros((1, LANES), F32)
    total1 = total0
    for k in range(len(messages)):
        tail = back_refs[k][groups * capacity : groups * capacity + 16, :][:, :capacity]
        seen = jnp.dot(tail, picks[k], preferred_element_type=F32)
        value = seen[0:1, :] + seen[1:2, :]
        total0 = total0 + jnp.where(first[k : k + 1, :], value, 0.0)
        total1 = total1 + jnp.where(second[k : k + 1, :], value, 0.0)
    comb = combine_ref[...].astype(F32)
    comb_ref[0:1, :] = total0 / comb[0:1, :]
    comb_ref[1:2, :] = total1 / comb[1:2, :]


def crossed(value, flips):
    experts, slots = lax.axis_size("expert"), lax.axis_size("dp")
    pairs = [
        (e * slots + d, (e ^ flips[d % 2]) * slots + d)
        for e in range(experts)
        for d in range(slots)
    ]
    return lax.ppermute(value, ("expert", "dp"), pairs)


def moved(value, message, back=False):
    shift, flip = message
    size = lax.axis_size("dp")
    chips = size // 2
    pairs = [(i, chip_after(i // 2, shift, chips) * 2 + (i % 2 ^ flip)) for i in range(size)]
    if back:
        pairs = sorted((b, a) for a, b in pairs)
    return lax.ppermute(value, "dp", pairs)


def vmem(mib):
    return pltpu.CompilerParams(vmem_limit_bytes=mib * 1024 * 1024)


def shape_of(*dims, dtype=BF16):
    return jax.ShapeDtypeStruct(dims, dtype)


def in_hbm(count):
    return [pl.BlockSpec(memory_space=HBM)] * count


def in_vmem(count):
    return [pl.BlockSpec(memory_space=pltpu.MemorySpace.VMEM)] * count


def kept_in_hbm(value):
    return pltpu.with_memory_space_constraint(value, HBM)


def anywhere(count):
    return [pl.BlockSpec(memory_space=pl.ANY)] * count


def run_hold(*weights):
    return pl.pallas_call(
        hold_kernel,
        in_specs=in_hbm(len(weights)),
        out_specs=in_vmem(len(weights)),
        out_shape=[shape_of(*value.shape) for value in weights],
        scratch_shapes=[pltpu.SemaphoreType.DMA((len(weights),))],
        compiler_params=vmem(16),
        cost_estimate=NO_COST,
    )(*map(kept_in_hbm, weights))


def run_relay(whole, *earlier):
    rows, width = whole.shape[0] // 2, whole.shape[1]
    return pl.pallas_call(
        functools.partial(relay_kernel, rows),
        in_specs=in_vmem(1) + anywhere(len(earlier)),
        out_specs=in_vmem(1)[0],
        out_shape=shape_of(rows, width),
        compiler_params=vmem(16),
        cost_estimate=NO_COST,
    )(whole, *earlier)


def run_forward(blocks, capacity, weights, *earlier):
    count = len(blocks)
    _, width, hidden = weights[0].shape
    return pl.pallas_call(
        functools.partial(forward_kernel, count, capacity, 256),
        in_specs=in_vmem(count + 3) + anywhere(len(earlier)),
        out_specs=in_vmem(1)[0],
        out_shape=shape_of(3, count * capacity, hidden),
        compiler_params=vmem(24),
        cost_estimate=NO_COST,
    )(*blocks, *weights, *earlier)


def run_backward(sums, count, capacity, w_gate, w_up, *earlier):
    _, width, hidden = w_gate.shape
    rows = count * capacity
    length = width // LANES * capacity + 16
    return pl.pallas_call(
        functools.partial(backward_kernel, count, capacity, 256),
        in_specs=in_vmem(4) + anywhere(len(earlier)),
        out_specs=in_vmem(3 + count),
        out_shape=[shape_of(rows, hidden)] * 3 + [shape_of(length, LANES)] * count,
        compiler_params=vmem(24),
        cost_estimate=NO_COST,
    )(*sums, w_gate, w_up, *earlier)


def run_weights(blocks, capacity, kept, hidden, *earlier):
    count, chunks = len(blocks), len(kept)
    width = blocks[0].shape[1]
    tile = 256
    column = pl.BlockSpec((2 * capacity, tile), lambda j: (0, j))
    flat = [kept[c][i] for i in range(3) for c in range(chunks)]
    held = [pl.BlockSpec(value.shape, lambda j: (0, 0)) for value in flat]
    row = pl.BlockSpec((1, tile, hidden), lambda j: (0, j, 0))
    return pl.pallas_call(
        functools.partial(weight_kernel, count, capacity, chunks),
        grid=(width // tile,),
        in_specs=[column] * count + held + anywhere(len(earlier)),
        out_specs=[row, row, pl.BlockSpec((1, hidden, tile), lambda j: (0, 0, j))],
        out_shape=[shape_of(1, width, hidden)] * 2 + [shape_of(1, hidden, width)],
        compiler_params=vmem(40),
        cost_estimate=NO_COST,
    )(*blocks, *flat, *earlier)


def expert_total(part, *earlier):
    got = crossed(part, (1, 2))
    if earlier:
        got = lax.optimization_barrier((got, *earlier))[0]
    pair = (part.astype(F32) + got.astype(F32)).astype(BF16)
    return pair, crossed(pair, (2, 1))


SHIFTS = (0, 3, 1, 2)
MESSAGES = tuple((shift, flip) for shift in SHIFTS for flip in (0, 1))


def after(value, *others):
    return lax.optimization_barrier((value, *others))[0]


def exchange_body(tokens, routes, combine, cotangent, w_gate, w_up, w_down):
    tok_rows, width = tokens.shape
    top_routes = routes.shape[1]
    experts = lax.axis_size("dp")
    capacity = 3 * tok_rows * top_routes // (2 * experts)
    hidden = w_gate.shape[2]
    routes_t, combine_t = routes.T, combine.T
    chunks = len(SHIFTS)
    sends = pl.pallas_call(
        functools.partial(send_kernel, MESSAGES, capacity, experts),
        in_specs=in_hbm(4),
        out_specs=in_vmem(chunks + 1),
        out_shape=[shape_of(2 * capacity, width)] * 2
        + [shape_of(4 * capacity, width)] * (chunks - 1),
        scratch_shapes=[
            pltpu.VMEM(routes_t.shape, jnp.int32),
            pltpu.VMEM(combine_t.shape, BF16),
            pltpu.VMEM(tokens.shape, BF16),
            pltpu.VMEM(tokens.shape, BF16),
            pltpu.SemaphoreType.DMA((4,)),
        ],
        compiler_params=vmem(32),
        cost_estimate=NO_COST,
    )(*map(kept_in_hbm, (routes_t, combine_t, tokens, cotangent)))
    weights = run_hold(w_gate, w_up, w_down)
    wholes = [sends[0]]
    for shift, value in zip(SHIFTS[1:], sends[2:]):
        wholes.append(moved(value, (shift, 0)))
    blocks, parts, sums, kept, backs = [], [], [], [], []

    def receive(i, *earlier):
        other = run_relay(wholes[i], *earlier) if i else sends[1]
        blocks.append((wholes[i], moved(other, (0, 1))))

    def forward(i, *earlier):
        parts.append(run_forward(blocks[i], capacity, weights, *earlier))

    def exchange(i, *earlier):
        sums.append(expert_total(parts[i], *earlier))

    def backward(i, *earlier):
        out = run_backward(sums[i], 2, capacity, *weights[:2], *earlier)
        kept.append(out[:3])
        for message, value in zip(MESSAGES[2 * i : 2 * i + 2], out[3:]):
            backs.append(value if message == (0, 0) else moved(value, message, back=True))

    receive(0)
    receive(1)
    forward(0)
    exchange(0)
    forward(1, sums[0][0])
    exchange(1)
    backward(0, parts[1])
    receive(2, kept[0][0])
    forward(2, sums[1][0], kept[0][0])
    exchange(2)
    backward(1, parts[2])
    receive(3, kept[1][0])
    forward(3, sums[2][0], kept[1][0])
    backward(2, parts[3])
    exchange(3, *backs[2:4], kept[2][0])
    backward(3, kept[2][0])
    flat = [block for pair in blocks for block in pair]
    grad_gate, grad_up, grad_down = run_weights(flat, capacity, kept, hidden)
    token_grad, comb_grad = pl.pallas_call(
        functools.partial(merge_kernel, MESSAGES, capacity, experts, 0),
        in_specs=in_vmem(2 + experts),
        out_specs=in_vmem(2),
        out_shape=[shape_of(tok_rows, width), shape_of(top_routes, tok_rows, dtype=F32)],
        compiler_params=vmem(32),
        cost_estimate=NO_COST,
    )(routes_t, combine_t, *backs)
    return (token_grad, comb_grad.T, grad_gate, grad_up, grad_down)


def gather_body(tokens, routes, combine, cotangent, w_gate, w_up, w_down):
    tok_rows, slice_width = tokens.shape
    top_routes = routes.shape[1]
    experts = lax.axis_size("dp")
    capacity = 3 * tok_rows * top_routes // (2 * experts)
    route_count = tok_rows * top_routes
    slot_total = experts * capacity
    route_flat = routes.reshape(route_count)
    onehot = (route_flat[:, None] == jnp.arange(experts, dtype=jnp.int32)[None, :]).astype(
        jnp.int32
    )
    slot_rank = jnp.sum((jnp.cumsum(onehot, axis=0) - onehot) * onehot, axis=1)
    places = route_flat * capacity + slot_rank
    source = jnp.full((slot_total,), route_count, jnp.int32)
    source = source.at[places].set(jnp.arange(route_count, dtype=jnp.int32))
    blank_row = jnp.zeros((1, slice_width), BF16)
    token_send = jnp.concatenate([tokens, blank_row], axis=0)[source // top_routes]
    cot_send = jnp.concatenate([cotangent, blank_row], axis=0)[source // top_routes]
    comb_send = jnp.concatenate(
        [combine.reshape(route_count), jnp.zeros((1,), BF16)], axis=0
    )[source]
    spread = functools.partial(
        lax.all_to_all, axis_name="dp", split_axis=0, concat_axis=0, tiled=True
    )
    token_slots = spread(token_send.reshape(experts, capacity, slice_width)).reshape(
        slot_total, slice_width
    )
    cot_slots = spread(cot_send.reshape(experts, capacity, slice_width)).reshape(
        slot_total, slice_width
    )
    comb_slots = spread(comb_send.reshape(experts, capacity)).reshape(slot_total).astype(F32)
    gate_mat, up_mat, down_mat = w_gate[0], w_up[0], w_down[0]
    partials = jnp.stack(
        [
            jnp.dot(token_slots, gate_mat, preferred_element_type=F32),
            jnp.dot(token_slots, up_mat, preferred_element_type=F32),
            contract_last(cot_slots, down_mat),
        ],
        axis=1,
    )
    summed = lax.psum_scatter(
        partials.astype(BF16), "expert", scatter_dimension=2, tiled=True
    ).astype(F32)
    hidden_part, gate_part, up_part = swiglu_grads(
        summed[:, 0], summed[:, 1], summed[:, 2], comb_slots
    )
    slot_comb = jnp.sum(hidden_part.astype(F32) * summed[:, 2], axis=1)
    joined = lax.all_gather(
        jnp.stack([hidden_part, gate_part, up_part], axis=1), "expert", axis=2, tiled=True
    )
    hidden, grad_gate_pre, grad_up_pre = joined[:, 0], joined[:, 1], joined[:, 2]
    slot_dx = contract_last(grad_gate_pre, gate_mat) + contract_last(grad_up_pre, up_mat)
    scaled_dy = (comb_slots[:, None] * cot_slots.astype(F32)).astype(BF16)
    grad_gate = contract_first(token_slots, grad_gate_pre).astype(BF16)[None]
    grad_up = contract_first(token_slots, grad_up_pre).astype(BF16)[None]
    grad_down = contract_first(hidden, scaled_dy).astype(BF16)[None]
    back_dx = spread(slot_dx.reshape(experts, capacity, slice_width).astype(BF16)).astype(F32)
    back_comb = spread(slot_comb.reshape(experts, capacity).astype(BF16)).astype(F32)
    route_dx = back_dx.reshape(slot_total, slice_width)[places].reshape(
        tok_rows, top_routes, slice_width
    )
    token_grad = jnp.sum(route_dx, axis=1).astype(BF16)
    comb_part = back_comb.reshape(slot_total)[places].reshape(tok_rows, top_routes)
    combine_grad = lax.psum(comb_part, "expert")
    return (token_grad, combine_grad, grad_gate, grad_up, grad_down)


def body(tokens, routes, combine, cotangent, w_gate, w_up, w_down):
    tok_rows, width = tokens.shape
    experts = lax.axis_size("dp")
    capacity = 3 * tok_rows * routes.shape[1] // (2 * experts)
    fits = (
        experts == 8
        and lax.axis_size("expert") == 4
        and routes.shape[1] == 2
        and tok_rows == LANES
        and capacity % 16 == 0
        and width % 256 == 0
        and w_gate.shape[2] % 256 == 0
    )
    run = exchange_body if fits else gather_body
    return run(tokens, routes, combine, cotangent, w_gate, w_up, w_down)


def solution(mesh):
    in_specs = (
        P("dp", "expert"),
        P("dp", None),
        P("dp", None),
        P("dp", "expert"),
        P("dp", "expert", None),
        P("dp", "expert", None),
        P("dp", None, "expert"),
    )
    out_specs = (
        P("dp", "expert"),
        P("dp", None),
        P("dp", "expert", None),
        P("dp", "expert", None),
        P("dp", None, "expert"),
    )
    return jax.shard_map(body, mesh=mesh, in_specs=in_specs, out_specs=out_specs, check_vma=False)
```
